32 devices in a mesh: tile: 16 (over z, y, x), mode: 2 (over core).
Axes of the slice: x: 2, y: 2, z: 4, core: 2. Of those that a mesh axis runs over, the one named last changes fastest.
Arguments:
- obj: float32 [16, 2, 384, 384], P('tile'), may hold values from -6 to 6
- probe: float32 [4, 2, 256, 256], P('mode'), may hold values from -3 to 3
- mode_weights: float32 [8, 4], P(None, 'mode'), may hold values from 0.25 to 1
- measured: float32 [64, 256, 256], P('tile'), may hold values from 0 to 4
- corner: int32 [64, 2], P('tile'), may hold values from 0 to 383, as said below
- counts: int32 [16], P('tile'), may hold values from 1 to 4, 32 in all
- weight_index: int32 [64], P('tile'), may hold values from 0 to 7
Outputs:
- obj_new: float32 [16, 2, 384, 384], P('tile')
- probe_new: float32 [4, 2, 256, 256], P('mode')
The draws below stay inside these ranges and needn't reach their ends.
Inputs may be any that keep to these rules, and one draw needn't show every extreme that they name: Tile t has live slots 0 to counts[t] - 1 of its block; the counts sum to 32 and some tile has 4. The first slot of every tile has both corner coordinates between 192 and 320.
All inputs are finite; a program needn't handle non-finite values.
Results may differ from the reference program's by a relative error of at most 0.019.
The reference program's roundings to bfloat16 on the way count: a program that leaves them out, or rounds other values in their place, can miss the bound.
Values may be sent and summed in bfloat16 or wider, within the bound.
No kernel may reach another device: no remote copies, remote signals or barrier semaphores. Data moves between devices by JAX's collectives and lax.ppermute only.
A program may use at most 64 MiB of HBM per device.

```python
import math
import jax
import jax.numpy as jnp
import numpy as np
from jax import lax

PATCH = 256
MODES = 4
KINDS = 8
GC = 8
TILE = 384
ITERS = 2
TILE_SLOT_LIMIT = 4
POSITIONS = 32
SLOTS = 64
N_TILE = 16


def draw_corner(key, part):
    first_key, second_key = jax.random.split(jax.random.fold_in(key, 17))
    spread = jax.random.randint(first_key, (SLOTS, 2), 0, TILE, dtype=jnp.int32)
    reaching = jax.random.randint(second_key, (SLOTS, 2), TILE - 3 * PATCH // 4, TILE - PATCH // 4 + 1, dtype=jnp.int32)
    leading = (jnp.arange(SLOTS, dtype=jnp.int32) % TILE_SLOT_LIMIT == 0)[:, None]
    result = jnp.where(leading, reaching, spread)
    result = result.at[1, 0].set(0)
    result = result.at[1, 1].set(TILE - 1)
    return result


def set_ends(values, rng, smallest, largest):
    spot = [jax.random.randint(jax.random.fold_in(rng, axis), (), 0, length) for axis, length in enumerate(values.shape)]
    longest = values.shape.index(max(values.shape))
    beside = spot[:longest] + [(spot[longest] + 1) % values.shape[longest]] + spot[longest + 1:]
    return values.at[tuple(spot)].set(smallest).at[tuple(beside)].set(largest)


def block_scale(rng, dims, pieces, smallest, top_value):
    def one(dim, blocks):
        steps = jax.random.uniform(jax.random.fold_in(jax.random.fold_in(rng, 6), dim), (blocks,), jnp.float32, smallest / len(pieces), top_value / len(pieces))
        return jnp.repeat(jnp.exp(steps), dims[dim] // blocks).reshape((-1,) + (1,) * (len(dims) - dim - 1))

    gain = one(*pieces[0])
    for cut in pieces[1:]:
        gain = gain * one(*cut)
    return gain


def length_profile(number_of, total, most, skew):
    loads = [(1 << 20) // math.isqrt(grade ** skew) + 1 for grade in range(2, number_of + 1)]
    spare, given = total - most - (number_of - 1), [1] * (number_of - 1)
    while spare > 0:
        candidates = [i for i in range(number_of - 1) if given[i] < most]
        mass, remaining = sum([loads[i] for i in candidates]), spare
        for i in candidates:
            more = min(most - given[i], max(1, remaining * loads[i] // mass), spare)
            given[i] = given[i] + more
            spare = spare - more
    return np.array([most] + given)


def uneven(rng, number_of, total, reach, lean):
    if number_of == 2:
        one = jax.random.randint(rng, (), max(1, total - reach), min(reach, total - 1) + 1)
        return jnp.stack([one, total - one])
    tallies = jnp.asarray(length_profile(number_of, total, reach, lean), jnp.int32)
    pairs = (number_of - 1) // 2
    giver, sink = tallies[1:1 + 2 * pairs:2], tallies[2:2 + 2 * pairs:2]
    room = jnp.minimum(giver - 1, reach - sink)
    passed = jax.random.randint(jax.random.fold_in(rng, 1), (pairs,), 0, 1 << 20) % (room + 1)
    tallies = tallies.at[1:1 + 2 * pairs:2].set(giver - passed).at[2:2 + 2 * pairs:2].set(sink + passed)
    return tallies[jax.random.permutation(jax.random.fold_in(rng, 2), number_of)]


def centred(own_key, dims, deviation, bound, pieces=(), held_as=jnp.bfloat16):
    entries = deviation * jax.random.normal(own_key, dims, jnp.float32)
    if pieces:
        entries = entries * block_scale(own_key, dims, pieces, -0.22, 0.18)
    return jnp.clip(entries, -bound, bound).astype(held_as)


def setup_inputs(seed: int = 0) -> dict:
    key_list = jax.random.split(jax.random.key(seed), 8)
    obj = centred(key_list[0], (N_TILE, 2, TILE, TILE), 1.0, 6.0, ((0, 16),), jnp.float32)
    probe = centred(key_list[1], (MODES, 2, PATCH, PATCH), 0.5, 3.0, ((0, 2),), jnp.float32)
    mode_weights = jnp.clip(jnp.exp(math.log(1.0) - 1.3862944 * jax.random.uniform(key_list[2], (KINDS, MODES), jnp.float32) ** block_scale(key_list[2], (KINDS, MODES), ((1, 2),), -0.2, 0.2)), 0.25, 1.0)
    measured = jnp.clip(4.0 * jax.random.uniform(key_list[3], (SLOTS, PATCH, PATCH), jnp.float32) ** block_scale(key_list[3], (SLOTS, PATCH, PATCH), ((0, 16),), -0.2, 0.2), 0.0, 4.0)
    corner = draw_corner(jax.random.fold_in(key_list[7], 71), 0)
    counts = uneven(key_list[5], N_TILE, POSITIONS, TILE_SLOT_LIMIT, 2).astype(jnp.int32)
    weight_index = set_ends(jax.random.randint(key_list[6], (SLOTS,), 0, KINDS), jax.random.fold_in(key_list[6], 1), 0, KINDS - 1).astype(jnp.int32)
    return {"obj": obj, "probe": probe, "mode_weights": mode_weights, "measured": measured, "corner": corner, "counts": counts, "weight_index": weight_index}


def dft_tables(length, sign):
    index = jnp.arange(length, dtype=jnp.int32)
    product = index[:, None] * index[None, :] % length
    angle = product.astype(jnp.float32) * (2.0 * math.pi / length)
    factor = 1.0 / math.sqrt(length)
    real = jnp.cos(angle) * factor
    imag = sign * jnp.sin(angle) * factor
    left = jnp.concatenate([jnp.concatenate([real, -imag], 1), jnp.concatenate([imag, real], 1)], 0).astype(jnp.bfloat16)
    right = jnp.concatenate([real, imag], 1).astype(jnp.bfloat16)
    return (left, right)

def transform(field, tables):
    left, right = tables
    count = field.shape[0]
    length = field.shape[-1]
    first = jnp.einsum('ij,bjk->bik', left.astype(jnp.float32), field.reshape(count, 2 * length, length).astype(jnp.float32))
    first = first.astype(jnp.bfloat16).reshape(count, 2, length, length)
    second = jnp.einsum('bcjk,kl->bcjl', first.astype(jnp.float32), right.astype(jnp.float32))
    real = second[:, 0, :, :length] - second[:, 1, :, length:]
    imag = second[:, 0, :, length:] + second[:, 1, :, :length]
    return jnp.stack([real, imag], 1)

def patch_contributions(object_patches, measured, active_mask, mode_weighting, probe, forward_pass, backward_pass):
    count = object_patches.shape[0]
    modes = probe.shape[0]
    length = probe.shape[-1]
    obj_part = object_patches.astype(jnp.float32)[:, None]
    probe_part = probe[None]
    exit_real = probe_part[:, :, 0] * obj_part[:, :, 0] - probe_part[:, :, 1] * obj_part[:, :, 1]
    exit_imag = probe_part[:, :, 0] * obj_part[:, :, 1] + probe_part[:, :, 1] * obj_part[:, :, 0]
    exit_wave = jnp.stack([exit_real, exit_imag], 2).astype(jnp.bfloat16)
    psi = transform(exit_wave.reshape(count * modes, 2, length, length), forward_pass).reshape(count, modes, 2, length, length)
    power = psi[:, :, 0] * psi[:, :, 0] + psi[:, :, 1] * psi[:, :, 1]
    intensity = lax.optimization_barrier(jnp.sum(mode_weighting[:, :, None, None] * power, 1))
    resid = (intensity - measured) * active_mask[:, None, None]
    scaled = (mode_weighting[:, :, None, None, None] * resid[:, None, None] * psi).astype(jnp.bfloat16)
    chi = transform(scaled.reshape(count * modes, 2, length, length), backward_pass).reshape(count, modes, 2, length, length)
    obj_real = lax.optimization_barrier(jnp.sum(probe_part[:, :, 0] * chi[:, :, 0] + probe_part[:, :, 1] * chi[:, :, 1], 1))
    obj_imag = lax.optimization_barrier(jnp.sum(probe_part[:, :, 0] * chi[:, :, 1] - probe_part[:, :, 1] * chi[:, :, 0], 1))
    probe_real = lax.optimization_barrier(jnp.sum(obj_part[:, :, 0] * chi[:, :, 0] + obj_part[:, :, 1] * chi[:, :, 1], 0))
    probe_imag = lax.optimization_barrier(jnp.sum(obj_part[:, :, 0] * chi[:, :, 1] - obj_part[:, :, 1] * chi[:, :, 0], 0))
    return (jnp.stack([obj_real, obj_imag], 1), jnp.stack([probe_real, probe_imag], 1))

def reference(obj, probe, mode_weights, measured, corner, counts, weight_index):
    forward_pass = dft_tables(PATCH, -1.0)
    backward_pass = dft_tables(PATCH, 1.0)
    zero_index = jnp.zeros((), jnp.int32)
    for sweep in range(ITERS):
        half = obj.astype(jnp.bfloat16)

        def per_tile(carry, tile_id):
            grad_tiles, grad_probe = carry
            beside = (tile_id + 1) % N_TILE
            under = (tile_id + GC) % N_TILE
            diagonal = (tile_id + GC + 1) % N_TILE
            upper = jnp.concatenate([half[tile_id], half[beside][:, :, :PATCH]], 2)
            lower = jnp.concatenate([half[under][:, :PATCH, :], half[diagonal][:, :PATCH, :PATCH]], 2)
            framed = jnp.concatenate([upper, lower], 1)
            corner_start = (tile_id * TILE_SLOT_LIMIT).astype(jnp.int32)
            spots = lax.dynamic_slice_in_dim(corner, corner_start, TILE_SLOT_LIMIT, 0)

            def cut(spot):
                return lax.dynamic_slice(framed, (zero_index, spot[0], spot[1]), (2, PATCH, PATCH))
            object_patches = jax.vmap(cut)(spots)
            measured_amplitudes = lax.dynamic_slice_in_dim(measured, corner_start, TILE_SLOT_LIMIT, 0)
            kinds = lax.dynamic_slice_in_dim(weight_index, corner_start, TILE_SLOT_LIMIT, 0)
            mode_weighting = mode_weights[kinds]
            active_mask = (jnp.arange(TILE_SLOT_LIMIT, dtype=jnp.int32) < counts[tile_id]).astype(jnp.float32)
            object_terms, probe_updates = patch_contributions(object_patches, measured_amplitudes, active_mask, mode_weighting, probe, forward_pass, backward_pass)

            def place(slot, acc):
                where = (zero_index, spots[slot, 0], spots[slot, 1])
                current = lax.dynamic_slice(acc, where, (2, PATCH, PATCH))
                return lax.dynamic_update_slice(acc, current + object_terms[slot], where)
            local = lax.fori_loop(0, TILE_SLOT_LIMIT, place, jnp.zeros((2, TILE + PATCH, TILE + PATCH), jnp.float32))
            grad_tiles = grad_tiles.at[tile_id].add(local[:, :TILE, :TILE])
            grad_tiles = grad_tiles.at[beside, :, :, :PATCH].add(local[:, :TILE, TILE:])
            grad_tiles = grad_tiles.at[under, :, :PATCH, :].add(local[:, TILE:, :TILE])
            grad_tiles = grad_tiles.at[diagonal, :, :PATCH, :PATCH].add(local[:, TILE:, TILE:])
            return ((grad_tiles, grad_probe + probe_updates), None)
        start_tiles = jnp.zeros((N_TILE, 2, TILE, TILE), jnp.float32)
        start_probe = jnp.zeros((MODES, 2, PATCH, PATCH), jnp.float32)
        (grad_tiles, grad_probe), unused = lax.scan(per_tile, (start_tiles, start_probe), jnp.arange(N_TILE, dtype=jnp.int32))
        obj = obj - 0.1 * grad_tiles
        probe = probe - 4.0 / POSITIONS * grad_probe
    return (obj, probe)
```

```python
import functools
import math

import jax
import jax.numpy as jnp
from jax import lax
from jax.experimental import pallas as pl
from jax.experimental.pallas import tpu as pltpu
from jax.sharding import PartitionSpec as P

GC = 8
POS_DEV = 2
ITERS = 2
STRIP = 32

step_object = 0.1
step_probe = 4.0

f32 = jnp.float32
bf16 = jnp.bfloat16
VM = pl.BlockSpec(memory_space=pltpu.VMEM)
SM = pl.BlockSpec(memory_space=pltpu.SMEM)


def shifted(array, by):
    peers = lax.axis_size("tile")
    return lax.ppermute(array, "tile", [(i, (i + by) % peers) for i in range(peers)])


def flipped(array, mask):
    peers = lax.axis_size("tile")
    return lax.ppermute(array, "tile", [(i, i ^ mask) for i in range(peers)])


def swapped(array):
    return lax.ppermute(array, "mode", [(0, 1), (1, 0)])


def dft_tables(length):
    index = jnp.arange(length, dtype=jnp.int32)
    product = index[:, None] * index[None, :] % length
    angle = product.astype(f32) * (2.0 * math.pi / length)
    factor = 1.0 / math.sqrt(length)
    real = jnp.cos(angle) * factor
    imag = -(jnp.sin(angle) * factor)
    one = jnp.concatenate(
        [jnp.concatenate([real, -imag], 1), jnp.concatenate([imag, real], 1)], 0
    ).astype(bf16)
    two = jnp.concatenate(
        [jnp.concatenate([real, imag], 1), jnp.concatenate([-imag, real], 1)], 0
    ).astype(bf16)
    return one, two


def dot(a, b):
    return jnp.dot(a, b, preferred_element_type=f32)


def patch_kernel(
    info, corner, kind, wm, wo,
    tm, rm, bm, dm, to, ro, bo, do, meas, pm, po, one, two,
    keep, send, pgm, pgo,
    frame, grad, psi, xs, ts, orr, oii, term, acc,
):
    n = pm.shape[-1]
    t = tm.shape[-1]
    half = pm.shape[0]
    modes = 2 * half
    me = info[0]
    live = info[1]
    for plane, (a, b, c, d) in ((me, (tm, rm, bm, dm)), (1 - me, (to, ro, bo, do))):
        frame[plane, pl.ds(0, t), pl.ds(0, t)] = a[...].astype(f32)
        frame[plane, pl.ds(0, t), pl.ds(t, n)] = b[...].astype(f32)
        frame[plane, pl.ds(t, n), pl.ds(0, t)] = c[...].astype(f32)
        frame[plane, pl.ds(t, n), pl.ds(t, n)] = d[...].astype(f32)
    grad[...] = jnp.zeros_like(grad)
    acc[...] = jnp.zeros_like(acc)

    def probe_at(m, c, rows):
        ref = pm if m < half else po
        return ref[m % half, c, rows, :]

    def slot_body(g, carry):
        s = me + 2 * g

        @pl.when(s < live)
        def _():
            row = corner[s, 0]
            col = corner[s, 1]
            rb = pl.multiple_of(row // 8 * 8, 8)
            rr = row - rb
            cb = pl.multiple_of(col // 128 * 128, 128)
            cc = col - cb
            high, wide = n + 8, n + 128
            for p, out in ((0, orr), (1, oii)):
                win = frame[p, pl.ds(rb, high), pl.ds(cb, wide)]
                win = pltpu.roll(win, lax.rem(wide - cc, wide), 1)[:, :n]
                win = pltpu.roll(win, lax.rem(high - rr, high), 0)[:n]
                out[...] = win
            strips = [pl.ds(i * STRIP, STRIP) for i in range(n // STRIP)]
            lower = [pl.ds(n + i * STRIP, STRIP) for i in range(n // STRIP)]
            w = [wm[kind[s], m] if m < half else wo[kind[s], m - half] for m in range(modes)]
            for m in range(modes):
                for up, lo in zip(strips, lower):
                    a, b = orr[up, :], oii[up, :]
                    pr, pi = probe_at(m, 0, up), probe_at(m, 1, up)
                    xs[m, up, :] = (pr * a - pi * b).astype(bf16)
                    xs[m, lo, :] = (pr * b + pi * a).astype(bf16)
            for m in range(modes):
                y = dot(one[...], xs[m])
                ts[pl.ds(m * n, n), pl.ds(0, n)] = y[:n].astype(bf16)
                ts[pl.ds(m * n, n), pl.ds(n, n)] = y[n:].astype(bf16)
            psi[...] = dot(ts[...], two[...])
            for i, (up, lo) in enumerate(zip(strips, lower)):
                total = jnp.zeros((STRIP, n), f32)
                for m in range(modes):
                    rows = pl.ds(m * n + i * STRIP, STRIP)
                    a, b = psi[rows, pl.ds(0, n)], psi[rows, pl.ds(n, n)]
                    total = total + w[m] * (a * a + b * b)
                resid = total - meas[s, up, :]
                for m in range(modes):
                    rows = pl.ds(m * n + i * STRIP, STRIP)
                    scale = w[m] * resid
                    xs[m, up, :] = (scale * psi[rows, pl.ds(0, n)]).astype(bf16)
                    xs[m, lo, :] = (scale * psi[rows, pl.ds(n, n)]).astype(bf16)
            for m in range(modes):
                y = dot(two[...], xs[m])
                ts[pl.ds(m * n, n), pl.ds(0, n)] = y[:n].astype(bf16)
                ts[pl.ds(m * n, n), pl.ds(n, n)] = y[n:].astype(bf16)
            psi[...] = dot(ts[...], one[...])
            for i, up in enumerate(strips):
                a, b = orr[up, :], oii[up, :]
                tr = jnp.zeros((STRIP, n), f32)
                ti = jnp.zeros((STRIP, n), f32)
                for m in range(modes):
                    rows = pl.ds(m * n + i * STRIP, STRIP)
                    cr, ci = psi[rows, pl.ds(0, n)], psi[rows, pl.ds(n, n)]
                    pr, pi = probe_at(m, 0, up), probe_at(m, 1, up)
                    tr = tr + (pr * cr + pi * ci)
                    ti = ti + (pr * ci - pi * cr)
                    acc[m, 0, up, :] += a * cr + b * ci
                    acc[m, 1, up, :] += a * ci - b * cr
                term[0, up, pl.ds(0, n)] = tr
                term[1, up, pl.ds(0, n)] = ti
            for p in range(2):
                term[p, pl.ds(n, 8), :] = jnp.zeros((8, wide), f32)
                term[p, pl.ds(0, n), pl.ds(n, 128)] = jnp.zeros((n, 128), f32)
                moved = pltpu.roll(pltpu.roll(term[p], rr, 0), cc, 1)
                grad[p, pl.ds(rb, high), pl.ds(cb, wide)] += moved

        return carry

    lax.fori_loop(0, meas.shape[0] // 2, slot_body, 0)
    keep[...] = grad[me]
    send[...] = grad[1 - me].astype(bf16)
    for m in range(half):
        pgm[m] = acc[m]
        pgo[m] = acc[half + m].astype(bf16)


def patches(info, corner, kind, wm, wo, mine, other, meas, pm, po, one, two):
    n = pm.shape[-1]
    t = mine[0].shape[-1]
    f = n + t
    modes = 2 * pm.shape[0]
    return pl.pallas_call(
        patch_kernel,
        out_shape=(
            jax.ShapeDtypeStruct((f, f), f32),
            jax.ShapeDtypeStruct((f, f), bf16),
            jax.ShapeDtypeStruct(pm.shape, f32),
            jax.ShapeDtypeStruct(pm.shape, bf16),
        ),
        in_specs=[SM] * 5 + [VM] * 13,
        out_specs=(VM,) * 4,
        scratch_shapes=[
            pltpu.VMEM((2, f, f), f32),
            pltpu.VMEM((2, f, f), f32),
            pltpu.VMEM((modes * n, 2 * n), f32),
            pltpu.VMEM((modes, 2 * n, n), bf16),
            pltpu.VMEM((modes * n, 2 * n), bf16),
            pltpu.VMEM((n, n), f32),
            pltpu.VMEM((n, n), f32),
            pltpu.VMEM((2, n + 8, n + 128), f32),
            pltpu.VMEM((modes, 2, n, n), f32),
        ],
        compiler_params=pltpu.CompilerParams(vmem_limit_bytes=60 * 1024 * 1024),
        name="patch",
    )(info, corner, kind, wm, wo, *mine, *other, meas, pm, po, one, two)


def margin_kernel(keep, got, own, right, low, diag):
    t = own.shape[0]
    f = keep.shape[0]
    n = f - t
    own[...] = keep[:t, :t] + got[:t, :t].astype(f32)
    right[...] = (keep[:t, t:] + got[:t, t:].astype(f32)).astype(bf16)
    low[...] = (keep[t:, :t] + got[t:, :t].astype(f32)).astype(bf16)
    diag[...] = (keep[t:, t:] + got[t:, t:].astype(f32)).astype(bf16)


def margins(keep, got, t):
    n = keep.shape[0] - t
    return pl.pallas_call(
        margin_kernel,
        out_shape=(
            jax.ShapeDtypeStruct((t, t), f32),
            jax.ShapeDtypeStruct((t, n), bf16),
            jax.ShapeDtypeStruct((n, t), bf16),
            jax.ShapeDtypeStruct((n, n), bf16),
        ),
        in_specs=[VM] * 2,
        out_specs=(VM,) * 4,
        name="margin",
    )(keep, got)


def update_kernel(state, own, right, low, diag, new, half, hr, hl, hd):
    n = diag.shape[0]
    new[...] = own[...]
    new[:, :n] += right[...].astype(f32)
    new[:n, :] += low[...].astype(f32)
    new[:n, :n] += diag[...].astype(f32)
    value = state[...] - step_object * new[...]
    new[...] = value
    small = value.astype(bf16)
    half[...] = small
    hr[...] = small[:, :n]
    hl[...] = small[:n, :]
    hd[...] = small[:n, :n]


def update(state, own, right, low, diag):
    t = state.shape[0]
    n = diag.shape[0]
    return pl.pallas_call(
        update_kernel,
        out_shape=(
            jax.ShapeDtypeStruct((t, t), f32),
            jax.ShapeDtypeStruct((t, t), bf16),
            jax.ShapeDtypeStruct((t, n), bf16),
            jax.ShapeDtypeStruct((n, t), bf16),
            jax.ShapeDtypeStruct((n, n), bf16),
        ),
        in_specs=[VM] * 5,
        out_specs=(VM,) * 5,
        name="update",
    )(state, own, right, low, diag)


def tile_sum(part):
    peers = lax.axis_size("tile")
    shape = part.shape
    rows = part.reshape(peers, -1, shape[-1]).astype(bf16)
    got = lax.all_to_all(rows, "tile", 0, 0, tiled=True)
    mine = jnp.sum(got.astype(f32), 0).astype(bf16)
    wide = jnp.broadcast_to(mine[None], rows.shape)
    return lax.all_to_all(wide, "tile", 0, 0, tiled=True).reshape(shape)


def body(obj, probe, mode_weights, measured, corner, counts, weight_index):
    n = probe.shape[-1]
    t = obj.shape[-1]
    me = lax.axis_index("mode")
    one, two = dft_tables(n)
    positions = POS_DEV * lax.axis_size("tile")
    info = jnp.stack([me.astype(jnp.int32), counts[0]])
    state = lax.dynamic_index_in_dim(obj[0], me, 0, keepdims=False)
    rest = lax.dynamic_index_in_dim(obj[0], 1 - me, 0, keepdims=False).astype(bf16)
    half = state.astype(bf16)
    edges = (half[:, :n], half[:n, :], half[:n, :n])
    pm = probe
    po = swapped(probe)
    wm = mode_weights
    wo = swapped(mode_weights)
    for sweep in range(ITERS):
        right = shifted(edges[0], -1)
        low = shifted(edges[1], -GC)
        diag = shifted(edges[2], -(GC + 1))
        mine = (half, right, low, diag)
        other = (rest, swapped(right), swapped(low), swapped(diag))
        keep, send, pgm, pgo = patches(
            info, corner, weight_index, wm, wo, mine, other, measured, pm, po, one, two
        )
        probe_grad = tile_sum(pgm + swapped(pgo).astype(f32))
        own, right, low, diag = margins(keep, swapped(send), t)
        right = shifted(right, 1)
        low = shifted(low, GC)
        diag = shifted(diag, GC + 1)
        state, half, *edges = update(state, own, right, low, diag)
        rate = step_probe / positions
        pm = pm - rate * probe_grad.astype(f32)
        if sweep < ITERS - 1:
            rest = swapped(half)
            po = po - rate * swapped(probe_grad).astype(f32)
    rest = swapped(state)
    first = jnp.where(me == 0, state, rest)
    second = jnp.where(me == 0, rest, state)
    return (jnp.stack([first, second])[None], pm)


def solution(mesh):
    placed = (
        P("tile", None, None, None),
        P("mode", None, None, None),
        P(None, "mode"),
        P("tile", None, None),
        P("tile", None),
        P("tile"),
        P("tile"),
    )
    return jax.shard_map(
        body,
        mesh=mesh,
        in_specs=placed,
        out_specs=(P("tile", None, None, None), P("mode", None, None, None)),
        check_vma=False,
    )
```

```python
import functools
import math

import jax
import jax.numpy as jnp
from jax import lax
from jax.experimental import pallas as pl
from jax.experimental.pallas import tpu as pltpu
from jax.sharding import PartitionSpec as P

GC = 8
POS_DEV = 2
ITERS = 2
STRIP = 32

step_object = 0.1
step_probe = 4.0

f32 = jnp.float32
bf16 = jnp.bfloat16
VM = pl.BlockSpec(memory_space=pltpu.VMEM)
SM = pl.BlockSpec(memory_space=pltpu.SMEM)


def shifted(array, by):
    peers = lax.axis_size("tile")
    return lax.ppermute(array, "tile", [(i, (i + by) % peers) for i in range(peers)])


def flipped(array, mask):
    peers = lax.axis_size("tile")
    return lax.ppermute(array, "tile", [(i, i ^ mask) for i in range(peers)])


def swapped(array):
    return lax.ppermute(array, "mode", [(0, 1), (1, 0)])


def dft_tables(length):
    index = jnp.arange(length, dtype=jnp.int32)
    product = index[:, None] * index[None, :] % length
    angle = product.astype(f32) * (2.0 * math.pi / length)
    factor = 1.0 / math.sqrt(length)
    real = jnp.cos(angle) * factor
    imag = -(jnp.sin(angle) * factor)
    one = jnp.concatenate(
        [jnp.concatenate([real, -imag], 1), jnp.concatenate([imag, real], 1)], 0
    ).astype(bf16)
    two = jnp.concatenate(
        [jnp.concatenate([real, imag], 1), jnp.concatenate([-imag, real], 1)], 0
    ).astype(bf16)
    return one, two


def dot(a, b):
    return jnp.dot(a, b, preferred_element_type=f32)


LANES = 128


def blocks(t, n, refs):
    right, low, diag = refs
    return ((right, 0, t, t, n), (low, t, 0, n, t), (diag, t, t, n, n))


def packed_rows(t, n):
    return (t * n // LANES, n * t // LANES, n * n // LANES)


def patch_kernel(
    live, corner, kind, wm, wo,
    tm, rm, bm, dm, to, ro, bo, do, meas, pm, po, one, two,
    own_keep, own_send, edge_keep, edge_send, pgm, pgo,
    frame, grad, psi, xs, ts, orr, oii, term, acc,
):
    n = pm.shape[-1]
    t = tm.shape[-1]
    half = pm.shape[0]
    modes = 2 * half
    me = lax.axis_index("mode")
    for plane, (a, b, c, d) in ((me, (tm, rm, bm, dm)), (1 - me, (to, ro, bo, do))):
        frame[plane, pl.ds(0, t), pl.ds(0, t)] = a[...].astype(f32)
        for ref, top, left, high, wide in blocks(t, n, (b, c, d)):
            for k in range(wide // LANES):
                part = ref[pl.ds(k * high, high), :].astype(f32)
                frame[plane, pl.ds(top, high), pl.ds(left + k * LANES, LANES)] = part
    grad[...] = jnp.zeros_like(grad)
    acc[...] = jnp.zeros_like(acc)

    def probe_at(m, c, rows):
        ref = pm if m < half else po
        return ref[m % half, c, rows, :]

    def slot_body(g, carry):
        s = me + 2 * g

        @pl.when(s < live[0])
        def _():
            row = corner[0, s]
            col = corner[1, s]
            rb = pl.multiple_of(row // 8 * 8, 8)
            rr = row - rb
            cb = pl.multiple_of(col // 128 * 128, 128)
            cc = col - cb
            high, wide = n + 8, n + 128
            for p, out in ((0, orr), (1, oii)):
                win = frame[p, pl.ds(rb, high), pl.ds(cb, wide)]
                win = pltpu.roll(win, lax.rem(wide - cc, wide), 1)[:, :n]
                win = pltpu.roll(win, lax.rem(high - rr, high), 0)[:n]
                out[...] = win
            strips = [pl.ds(i * STRIP, STRIP) for i in range(n // STRIP)]
            lower = [pl.ds(n + i * STRIP, STRIP) for i in range(n // STRIP)]
            w = [wm[m, kind[s]] if m < half else wo[m - half, kind[s]] for m in range(modes)]
            for m in range(modes):
                for up, lo in zip(strips, lower):
                    a, b = orr[up, :], oii[up, :]
                    pr, pi = probe_at(m, 0, up), probe_at(m, 1, up)
                    xs[m, up, :] = (pr * a - pi * b).astype(bf16)
                    xs[m, lo, :] = (pr * b + pi * a).astype(bf16)
            for m in range(modes):
                y = dot(one[...], xs[m])
                ts[pl.ds(m * n, n), pl.ds(0, n)] = y[:n].astype(bf16)
                ts[pl.ds(m * n, n), pl.ds(n, n)] = y[n:].astype(bf16)
            psi[...] = dot(ts[...], two[...])
            for i, (up, lo) in enumerate(zip(strips, lower)):
                total = jnp.zeros((STRIP, n), f32)
                for m in range(modes):
                    rows = pl.ds(m * n + i * STRIP, STRIP)
                    a, b = psi[rows, pl.ds(0, n)], psi[rows, pl.ds(n, n)]
                    total = total + w[m] * (a * a + b * b)
                resid = total - meas[s, up, :]
                for m in range(modes):
                    rows = pl.ds(m * n + i * STRIP, STRIP)
                    scale = w[m] * resid
                    xs[m, up, :] = (scale * psi[rows, pl.ds(0, n)]).astype(bf16)
                    xs[m, lo, :] = (scale * psi[rows, pl.ds(n, n)]).astype(bf16)
            for m in range(modes):
                y = dot(two[...], xs[m])
                ts[pl.ds(m * n, n), pl.ds(0, n)] = y[:n].astype(bf16)
                ts[pl.ds(m * n, n), pl.ds(n, n)] = y[n:].astype(bf16)
            psi[...] = dot(ts[...], one[...])
            for i, up in enumerate(strips):
                a, b = orr[up, :], oii[up, :]
                tr = jnp.zeros((STRIP, n), f32)
                ti = jnp.zeros((STRIP, n), f32)
                for m in range(modes):
                    rows = pl.ds(m * n + i * STRIP, STRIP)
                    cr, ci = psi[rows, pl.ds(0, n)], psi[rows, pl.ds(n, n)]
                    pr, pi = probe_at(m, 0, up), probe_at(m, 1, up)
                    tr = tr + (pr * cr + pi * ci)
                    ti = ti + (pr * ci - pi * cr)
                    acc[m, 0, up, :] += a * cr + b * ci
                    acc[m, 1, up, :] += a * ci - b * cr
                term[0, up, pl.ds(0, n)] = tr
                term[1, up, pl.ds(0, n)] = ti
            for p in range(2):
                term[p, pl.ds(n, 8), :] = jnp.zeros((8, wide), f32)
                term[p, pl.ds(0, n), pl.ds(n, 128)] = jnp.zeros((n, 128), f32)
                moved = pltpu.roll(pltpu.roll(term[p], rr, 0), cc, 1)
                grad[p, pl.ds(rb, high), pl.ds(cb, wide)] += moved

        return carry

    lax.fori_loop(0, meas.shape[0] // 2, slot_body, 0)
    own_keep[...] = grad[me, pl.ds(0, t), pl.ds(0, t)]
    own_send[...] = grad[1 - me, pl.ds(0, t), pl.ds(0, t)].astype(bf16)
    base = 0
    for _, top, left, high, wide in blocks(t, n, (None,) * 3):
        for k in range(wide // LANES):
            rows, lanes = pl.ds(top, high), pl.ds(left + k * LANES, LANES)
            edge_keep[pl.ds(base, high), :] = grad[me, rows, lanes]
            edge_send[pl.ds(base, high), :] = grad[1 - me, rows, lanes].astype(bf16)
            base += high
    for m in range(half):
        pgm[m] = acc[m]
        pgo[m] = acc[half + m].astype(bf16)


def call(kernel, name, outs, *args, smem=1, scratch=(), limit=4 * 1024 * 1024):
    return pl.pallas_call(
        kernel,
        out_shape=tuple(jax.ShapeDtypeStruct(shape, dtype) for shape, dtype in outs),
        in_specs=[SM] * smem + [VM] * (len(args) - smem),
        out_specs=(VM,) * len(outs),
        scratch_shapes=list(scratch),
        compiler_params=pltpu.CompilerParams(vmem_limit_bytes=limit),
        name=name,
    )(*args)


def patches(live, corner, kind, wm, wo, mine, other, meas, pm, po, one, two):
    n = pm.shape[-1]
    t = mine[0].shape[-1]
    f = n + t
    modes = 2 * pm.shape[0]
    rows = sum(packed_rows(t, n))
    return call(
        patch_kernel,
        "patch",
        (
            ((t, t), f32),
            ((t, t), bf16),
            ((rows, LANES), f32),
            ((rows, LANES), bf16),
            (pm.shape, f32),
            (pm.shape, bf16),
        ),
        live, corner, kind, wm, wo, *mine, *other, meas, pm, po, one, two,
        smem=5,
        scratch=[
            pltpu.VMEM((2, f, f), f32),
            pltpu.VMEM((2, f, f), f32),
            pltpu.VMEM((modes * n, 2 * n), f32),
            pltpu.VMEM((modes, 2 * n, n), bf16),
            pltpu.VMEM((modes * n, 2 * n), bf16),
            pltpu.VMEM((n, n), f32),
            pltpu.VMEM((n, n), f32),
            pltpu.VMEM((2, n + 8, n + 128), f32),
            pltpu.VMEM((modes, 2, n, n), f32),
        ],
        limit=24 * 1024 * 1024,
    )


def pack_edges(value, t, n, outs):
    for out, _, _, high, wide in blocks(t, n, outs):
        for k in range(wide // LANES):
            out[pl.ds(k * high, high), :] = value[:high, k * LANES : (k + 1) * LANES]


def enter_kernel(obj, state, half, rest, hr, hl, hd):
    me = lax.axis_index("mode")
    t = obj.shape[-1]
    n = hl.shape[0] * LANES // t
    value = obj[me]
    state[...] = value
    small = value.astype(bf16)
    half[...] = small
    pack_edges(small, t, n, (hr, hl, hd))
    rest[...] = obj[1 - me].astype(bf16)


def edge_shapes(t, n):
    return tuple(((rows, LANES), bf16) for rows in packed_rows(t, n))


def enter(obj, n):
    t = obj.shape[-1]
    outs = (((t, t), f32), ((t, t), bf16), ((t, t), bf16)) + edge_shapes(t, n)
    return call(enter_kernel, "enter", outs, obj, smem=0, limit=4 * 1024 * 1024)


def margin_kernel(keep, got, right, low, diag):
    base = 0
    for out in (right, low, diag):
        rows = pl.ds(base, out.shape[0])
        out[...] = (keep[rows, :] + got[rows, :].astype(f32)).astype(bf16)
        base += out.shape[0]


def margins(keep, got, t, n):
    return call(margin_kernel, "margin", edge_shapes(t, n), keep, got, smem=0)


def update_kernel(state, keep, got, right, low, diag, new, half, hr, hl, hd):
    t = state.shape[0]
    n = low.shape[0] * LANES // t
    new[...] = keep[...] + got[...].astype(f32)
    for ref, _, _, high, wide in blocks(t, n, (right, low, diag)):
        for k in range(wide // LANES):
            lanes = pl.ds(k * LANES, LANES)
            new[pl.ds(0, high), lanes] += ref[pl.ds(k * high, high), :].astype(f32)
    value = state[...] - step_object * new[...]
    new[...] = value
    small = value.astype(bf16)
    half[...] = small
    pack_edges(small, t, n, (hr, hl, hd))


def update(state, keep, got, right, low, diag):
    t = state.shape[0]
    n = low.shape[0] * LANES // t
    outs = (((t, t), f32), ((t, t), bf16)) + edge_shapes(t, n)
    return call(update_kernel, "update", outs, state, keep, got, right, low, diag, smem=0, limit=4 * 1024 * 1024)


def leave_kernel(state, rest, out):
    me = lax.axis_index("mode")
    out[me] = state[...]
    out[1 - me] = rest[...]


def leave(state, rest):
    outs = (((2, *state.shape), f32),)
    return call(leave_kernel, "leave", outs, state, rest, smem=0)[0]


def digits(peers):
    out, shift = [], 0
    while 1 << shift < peers:
        radix = 4 if (4 << shift) <= peers else 2
        out.append((shift, radix))
        shift += radix.bit_length() - 1
    return out


def spot_of(shift, radix):
    return (lax.axis_index("tile") >> shift) & (radix - 1)


def first_kernel(place, keep, got, own, *sends):
    i = spot_of(*place)
    own[...] = keep[i] + got[i].astype(f32)
    for k, out in enumerate(sends):
        j = i ^ (k + 1)
        out[...] = (keep[j] + got[j].astype(f32)).astype(bf16)


def stage_kernel(before, place, have, *refs):
    after = place[1]
    got = refs[: before - 1]
    own, sends = refs[before - 1], refs[before:]
    total = refs[-1]
    sends = sends[:-1]
    value = have[...]
    for ref in got:
        value = value + ref[...].astype(f32)
    if after == 1:
        own[...] = value.astype(bf16)
        return
    total[...] = value
    rows = own.shape[0]
    i = spot_of(*place)
    own[...] = total[pl.ds(pl.multiple_of(i * rows, rows), rows), :]
    for k, out in enumerate(sends):
        j = i ^ (k + 1)
        out[...] = total[pl.ds(pl.multiple_of(j * rows, rows), rows), :].astype(bf16)


def join_kernel(place, have, *refs):
    got, out = refs[:-1], refs[-1]
    rows = have.shape[0]
    i = spot_of(*place)
    out[pl.ds(pl.multiple_of(i * rows, rows), rows), :] = have[...]
    for k, ref in enumerate(got):
        j = i ^ (k + 1)
        out[pl.ds(pl.multiple_of(j * rows, rows), rows), :] = ref[...]


def apply_kernel(rate, place, probe, have, *refs):
    got, out = refs[:-1], refs[-1]
    i = spot_of(*place)
    for k, ref in enumerate((have, *got)):
        j = i ^ k
        out[j] = probe[j] - rate * ref[...].astype(f32)


def probe_sum(keep, got):
    n = keep.shape[-1]
    stages = digits(lax.axis_size("tile"))
    shift, radix = stages[0]
    keep = keep.reshape(radix, -1, n)
    got = got.reshape(keep.shape)
    rows = keep.shape[1]
    own, *sends = call(
        functools.partial(first_kernel, (shift, radix)),
        "first",
        (((rows, n), f32),) + (((rows, n), bf16),) * (radix - 1),
        keep, got, smem=0,
    )
    for at, (shift, radix) in enumerate(stages):
        got = [flipped(part, (k + 1) << shift) for k, part in enumerate(sends)]
        if at + 1 < len(stages):
            place = stages[at + 1]
            small = rows // place[1]
            outs = (((small, n), f32),) + (((small, n), bf16),) * (place[1] - 1)
        else:
            place, small = (0, 1), rows
            outs = (((rows, n), bf16),)
        own, *sends = call(
            functools.partial(stage_kernel, radix, place),
            "stage", outs, own, *got, smem=0,
            scratch=[pltpu.VMEM((rows, n), f32)],
        )
        rows = small
    for at, (shift, radix) in reversed(list(enumerate(stages))):
        got = [flipped(own, k << shift) for k in range(1, radix)]
        if at:
            outs = (((rows * radix, n), bf16),)
            join = functools.partial(join_kernel, (shift, radix))
            (own,) = call(join, "join", outs, own, *got, smem=0)
            rows = rows * radix
    return (own, *got)


def probe_step(rate, probe, pieces):
    place = digits(lax.axis_size("tile"))[0]
    chunks = probe.reshape(place[1], -1, probe.shape[-1])
    (out,) = call(
        functools.partial(apply_kernel, rate, place),
        "apply", ((chunks.shape, f32),), chunks, *pieces, smem=0,
    )
    return out.reshape(probe.shape)


def body(obj, probe, mode_weights, measured, corner, counts, weight_index):
    n = probe.shape[-1]
    t = obj.shape[-1]
    one, two = dft_tables(n)
    rate = step_probe / (POS_DEV * lax.axis_size("tile"))
    state, half, rest, *edges = enter(obj[0], n)
    pm = probe
    po = swapped(probe)
    wm = mode_weights.T
    wo = swapped(wm)
    spots = corner.T
    for sweep in range(ITERS):
        low = shifted(edges[1], -GC)
        diag = shifted(edges[2], -(GC + 1))
        right = shifted(edges[0], -1)
        mine = (half, right, low, diag)
        other = (rest, swapped(right), swapped(low), swapped(diag))
        own_keep, own_send, edge_keep, edge_send, pgm, pgo = patches(
            counts, spots, weight_index, wm, wo, mine, other, measured, pm, po, one, two
        )
        right, low, diag = margins(edge_keep, swapped(edge_send), t, n)
        low = shifted(low, GC)
        diag = shifted(diag, GC + 1)
        right = shifted(right, 1)
        pieces = probe_sum(pgm, swapped(pgo))
        state, half, *edges = update(state, own_keep, swapped(own_send), right, low, diag)
        pm = probe_step(rate, pm, pieces)
        if sweep < ITERS - 1:
            rest = swapped(half)
            po = probe_step(rate, po, [swapped(piece) for piece in pieces])
    return (leave(state, swapped(state))[None], pm)


def solution(mesh):
    placed = (
        P("tile", None, None, None),
        P("mode", None, None, None),
        P(None, "mode"),
        P("tile", None, None),
        P("tile", None),
        P("tile"),
        P("tile"),
    )
    return jax.shard_map(
        body,
        mesh=mesh,
        in_specs=placed,
        out_specs=(P("tile", None, None, None), P("mode", None, None, None)),
        check_vma=False,
    )
```

```python
import functools
import math

import jax
import jax.numpy as jnp
from jax import lax
from jax.experimental import pallas as pl
from jax.experimental.pallas import tpu as pltpu
from jax.sharding import PartitionSpec as P


GC = 8
POS_DEV = 2
ITERS = 2
STRIP = 32

step_object = 0.1
step_probe = 4.0

f32 = jnp.float32
bf16 = jnp.bfloat16
VM = pl.BlockSpec(memory_space=pltpu.VMEM)
SM = pl.BlockSpec(memory_space=pltpu.SMEM)


def shifted(array, by):
    peers = lax.axis_size("tile")
    return lax.ppermute(array, "tile", [(i, (i + by) % peers) for i in range(peers)])


def flipped(array, mask):
    peers = lax.axis_size("tile")
    return lax.ppermute(array, "tile", [(i, i ^ mask) for i in range(peers)])


def swapped(array):
    return lax.ppermute(array, "mode", [(0, 1), (1, 0)])


def dft_tables(length):
    index = jnp.arange(length, dtype=jnp.int32)
    product = index[:, None] * index[None, :] % length
    angle = product.astype(f32) * (2.0 * math.pi / length)
    factor = 1.0 / math.sqrt(length)
    real = jnp.cos(angle) * factor
    imag = -(jnp.sin(angle) * factor)
    one = jnp.concatenate(
        [jnp.concatenate([real, -imag], 1), jnp.concatenate([imag, real], 1)], 0
    ).astype(bf16)
    two = jnp.concatenate(
        [jnp.concatenate([real, imag], 1), jnp.concatenate([-imag, real], 1)], 0
    ).astype(bf16)
    return one, two


def dot(a, b):
    return jnp.dot(a, b, preferred_element_type=f32)


LANES = 128


def blocks(t, n, refs):
    right, low, diag = refs
    return ((right, 0, t, t, n), (low, t, 0, n, t), (diag, t, t, n, n))


def packed_rows(t, n):
    return (t * n // LANES, n * t // LANES, n * n // LANES)


def patch_kernel(
    live, corner, kind, wm, wo,
    tm, rm, bm, dm, to, ro, bo, do, meas, pm, po, one, two,
    own_keep, own_send, edge_keep, edge_send, pgm, pgo,
    frame, grad, psi, xs, ts, orr, oii, term, acc,
):
    n = pm.shape[-1]
    t = tm.shape[-1]
    half = pm.shape[0]
    modes = 2 * half
    me = lax.axis_index("mode")
    for plane, (a, b, c, d) in ((me, (tm, rm, bm, dm)), (1 - me, (to, ro, bo, do))):
        frame[plane, pl.ds(0, t), pl.ds(0, t)] = a[...].astype(f32)
        for ref, top, left, high, wide in blocks(t, n, (b, c, d)):
            for k in range(wide // LANES):
                part = ref[pl.ds(k * high, high), :].astype(f32)
                frame[plane, pl.ds(top, high), pl.ds(left + k * LANES, LANES)] = part
    grad[...] = jnp.zeros_like(grad)
    acc[...] = jnp.zeros_like(acc)

    def probe_at(m, c, rows):
        ref = pm if m < half else po
        return ref[m % half, c, rows, :]

    def slot_body(g, carry):
        s = me + 2 * g

        @pl.when(s < live[0])
        def _():
            row = corner[0, s]
            col = corner[1, s]
            rb = pl.multiple_of(row // 8 * 8, 8)
            rr = row - rb
            cb = pl.multiple_of(col // 128 * 128, 128)
            cc = col - cb
            high, wide = n + 8, n + 128
            for p, out in ((0, orr), (1, oii)):
                win = frame[p, pl.ds(rb, high), pl.ds(cb, wide)]
                win = pltpu.roll(win, lax.rem(wide - cc, wide), 1)[:, :n]
                win = pltpu.roll(win, lax.rem(high - rr, high), 0)[:n]
                out[...] = win
            strips = [pl.ds(i * STRIP, STRIP) for i in range(n // STRIP)]
            lower = [pl.ds(n + i * STRIP, STRIP) for i in range(n // STRIP)]
            w = [wm[m, kind[s]] if m < half else wo[m - half, kind[s]] for m in range(modes)]
            for m in range(modes):
                for up, lo in zip(strips, lower):
                    a, b = orr[up, :], oii[up, :]
                    pr, pi = probe_at(m, 0, up), probe_at(m, 1, up)
                    xs[m, up, :] = (pr * a - pi * b).astype(bf16)
                    xs[m, lo, :] = (pr * b + pi * a).astype(bf16)
            for m in range(modes):
                y = dot(one[...], xs[m])
                ts[pl.ds(m * n, n), pl.ds(0, n)] = y[:n].astype(bf16)
                ts[pl.ds(m * n, n), pl.ds(n, n)] = y[n:].astype(bf16)
            psi[...] = dot(ts[...], two[...])
            for i, (up, lo) in enumerate(zip(strips, lower)):
                total = jnp.zeros((STRIP, n), f32)
                for m in range(modes):
                    rows = pl.ds(m * n + i * STRIP, STRIP)
                    a, b = psi[rows, pl.ds(0, n)], psi[rows, pl.ds(n, n)]
                    total = total + w[m] * (a * a + b * b)
                resid = total - meas[s, up, :]
                for m in range(modes):
                    rows = pl.ds(m * n + i * STRIP, STRIP)
                    scale = w[m] * resid
                    xs[m, up, :] = (scale * psi[rows, pl.ds(0, n)]).astype(bf16)
                    xs[m, lo, :] = (scale * psi[rows, pl.ds(n, n)]).astype(bf16)
            for m in range(modes):
                y = dot(two[...], xs[m])
                ts[pl.ds(m * n, n), pl.ds(0, n)] = y[:n].astype(bf16)
                ts[pl.ds(m * n, n), pl.ds(n, n)] = y[n:].astype(bf16)
            psi[...] = dot(ts[...], one[...])
            for i, up in enumerate(strips):
                a, b = orr[up, :], oii[up, :]
                tr = jnp.zeros((STRIP, n), f32)
                ti = jnp.zeros((STRIP, n), f32)
                for m in range(modes):
                    rows = pl.ds(m * n + i * STRIP, STRIP)
                    cr, ci = psi[rows, pl.ds(0, n)], psi[rows, pl.ds(n, n)]
                    pr, pi = probe_at(m, 0, up), probe_at(m, 1, up)
                    tr = tr + (pr * cr + pi * ci)
                    ti = ti + (pr * ci - pi * cr)
                    acc[m, 0, up, :] += a * cr + b * ci
                    acc[m, 1, up, :] += a * ci - b * cr
                term[0, up, pl.ds(0, n)] = tr
                term[1, up, pl.ds(0, n)] = ti
            for p in range(2):
                term[p, pl.ds(n, 8), :] = jnp.zeros((8, wide), f32)
                term[p, pl.ds(0, n), pl.ds(n, 128)] = jnp.zeros((n, 128), f32)
                moved = pltpu.roll(pltpu.roll(term[p], rr, 0), cc, 1)
                grad[p, pl.ds(rb, high), pl.ds(cb, wide)] += moved

        return carry

    lax.fori_loop(0, meas.shape[0] // 2, slot_body, 0)
    own_keep[...] = grad[me, pl.ds(0, t), pl.ds(0, t)]
    own_send[...] = grad[1 - me, pl.ds(0, t), pl.ds(0, t)].astype(bf16)
    base = 0
    for _, top, left, high, wide in blocks(t, n, (None,) * 3):
        for k in range(wide // LANES):
            rows, lanes = pl.ds(top, high), pl.ds(left + k * LANES, LANES)
            edge_keep[pl.ds(base, high), :] = grad[me, rows, lanes]
            edge_send[pl.ds(base, high), :] = grad[1 - me, rows, lanes].astype(bf16)
            base += high
    for m in range(half):
        pgm[m] = acc[m]
        pgo[m] = acc[half + m].astype(bf16)


def call(kernel, outs, *args, smem=0, scratch=(), limit=4 * 1024 * 1024):
    return pl.pallas_call(
        kernel,
        out_shape=tuple(jax.ShapeDtypeStruct(shape, dtype) for shape, dtype in outs),
        in_specs=[SM] * smem + [VM] * (len(args) - smem),
        out_specs=(VM,) * len(outs),
        scratch_shapes=list(scratch),
        compiler_params=pltpu.CompilerParams(vmem_limit_bytes=limit),
        name="kernel",
    )(*args)


def patches(live, corner, kind, wm, wo, mine, other, meas, pm, po, one, two):
    n = pm.shape[-1]
    t = mine[0].shape[-1]
    f = n + t
    modes = 2 * pm.shape[0]
    rows = sum(packed_rows(t, n))
    return call(
        patch_kernel,
        (
            ((t, t), f32),
            ((t, t), bf16),
            ((rows, LANES), f32),
            ((rows, LANES), bf16),
            (pm.shape, f32),
            (pm.shape, bf16),
        ),
        live, corner, kind, wm, wo, *mine, *other, meas, pm, po, one, two,
        smem=5,
        scratch=[
            pltpu.VMEM((2, f, f), f32),
            pltpu.VMEM((2, f, f), f32),
            pltpu.VMEM((modes * n, 2 * n), f32),
            pltpu.VMEM((modes, 2 * n, n), bf16),
            pltpu.VMEM((modes * n, 2 * n), bf16),
            pltpu.VMEM((n, n), f32),
            pltpu.VMEM((n, n), f32),
            pltpu.VMEM((2, n + 8, n + 128), f32),
            pltpu.VMEM((modes, 2, n, n), f32),
        ],
        limit=24 * 1024 * 1024,
    )


def pack_edges(value, t, n, outs):
    for out, _, _, high, wide in blocks(t, n, outs):
        for k in range(wide // LANES):
            out[pl.ds(k * high, high), :] = value[:high, k * LANES : (k + 1) * LANES]


def enter_kernel(obj, state, half, rest, hr, hl, hd):
    me = lax.axis_index("mode")
    t = obj.shape[-1]
    n = hl.shape[0] * LANES // t
    value = obj[me]
    state[...] = value
    small = value.astype(bf16)
    half[...] = small
    pack_edges(small, t, n, (hr, hl, hd))
    rest[...] = obj[1 - me].astype(bf16)


def edge_shapes(t, n):
    return tuple(((rows, LANES), bf16) for rows in packed_rows(t, n))


def enter(obj, n):
    t = obj.shape[-1]
    outs = (((t, t), f32), ((t, t), bf16), ((t, t), bf16)) + edge_shapes(t, n)
    return call(enter_kernel, outs, obj)


def margin_kernel(keep, got, right, low, diag):
    base = 0
    for out in (right, low, diag):
        rows = pl.ds(base, out.shape[0])
        out[...] = (keep[rows, :] + got[rows, :].astype(f32)).astype(bf16)
        base += out.shape[0]


def margins(keep, got, t, n):
    return call(margin_kernel, edge_shapes(t, n), keep, got)


def update_kernel(state, keep, got, right, low, diag, new, half, hr, hl, hd):
    t = state.shape[0]
    n = low.shape[0] * LANES // t
    new[...] = keep[...] + got[...].astype(f32)
    for ref, _, _, high, wide in blocks(t, n, (right, low, diag)):
        for k in range(wide // LANES):
            lanes = pl.ds(k * LANES, LANES)
            new[pl.ds(0, high), lanes] += ref[pl.ds(k * high, high), :].astype(f32)
    value = state[...] - step_object * new[...]
    new[...] = value
    small = value.astype(bf16)
    half[...] = small
    pack_edges(small, t, n, (hr, hl, hd))


def update(state, keep, got, right, low, diag):
    t = state.shape[0]
    n = low.shape[0] * LANES // t
    outs = (((t, t), f32), ((t, t), bf16)) + edge_shapes(t, n)
    return call(update_kernel, outs, state, keep, got, right, low, diag)


def leave_kernel(state, rest, out):
    me = lax.axis_index("mode")
    out[me] = state[...]
    out[1 - me] = rest[...]


def leave(state, rest):
    outs = (((2, *state.shape), f32),)
    return call(leave_kernel, outs, state, rest)[0]


def digits(peers):
    out, shift = [], 0
    while 1 << shift < peers:
        radix = 4 if (4 << shift) <= peers else 2
        out.append((shift, radix))
        shift += radix.bit_length() - 1
    return out


def spot_of(shift, radix):
    return (lax.axis_index("tile") >> shift) & (radix - 1)


def first_kernel(place, keep, got, own, *sends):
    i = spot_of(*place)
    own[...] = keep[i] + got[i].astype(f32)
    for k, out in enumerate(sends):
        j = i ^ (k + 1)
        out[...] = (keep[j] + got[j].astype(f32)).astype(bf16)


def stage_kernel(before, place, have, *refs):
    after = place[1]
    got = refs[: before - 1]
    own, sends = refs[before - 1], refs[before:]
    total = refs[-1]
    sends = sends[:-1]
    value = have[...]
    for ref in got:
        value = value + ref[...].astype(f32)
    if after == 1:
        own[...] = value.astype(bf16)
        return
    total[...] = value
    rows = own.shape[0]
    i = spot_of(*place)
    own[...] = total[pl.ds(pl.multiple_of(i * rows, rows), rows), :]
    for k, out in enumerate(sends):
        j = i ^ (k + 1)
        out[...] = total[pl.ds(pl.multiple_of(j * rows, rows), rows), :].astype(bf16)


def join_kernel(place, have, *refs):
    got, out = refs[:-1], refs[-1]
    rows = have.shape[0]
    i = spot_of(*place)
    out[pl.ds(pl.multiple_of(i * rows, rows), rows), :] = have[...]
    for k, ref in enumerate(got):
        j = i ^ (k + 1)
        out[pl.ds(pl.multiple_of(j * rows, rows), rows), :] = ref[...]


def apply_kernel(rate, place, probe, have, *refs):
    got, out = refs[:-1], refs[-1]
    i = spot_of(*place)
    for k, ref in enumerate((have, *got)):
        j = i ^ k
        out[j] = probe[j] - rate * ref[...].astype(f32)


def probe_sum(keep, got):
    n = keep.shape[-1]
    stages = digits(lax.axis_size("tile"))
    shift, radix = stages[0]
    keep = keep.reshape(radix, -1, n)
    got = got.reshape(keep.shape)
    rows = keep.shape[1]
    own, *sends = call(
        functools.partial(first_kernel, (shift, radix)),
        (((rows, n), f32),) + (((rows, n), bf16),) * (radix - 1),
        keep, got,
    )
    for at, (shift, radix) in enumerate(stages):
        got = [flipped(part, (k + 1) << shift) for k, part in enumerate(sends)]
        if at + 1 < len(stages):
            place = stages[at + 1]
            small = rows // place[1]
            outs = (((small, n), f32),) + (((small, n), bf16),) * (place[1] - 1)
        else:
            place, small = (0, 1), rows
            outs = (((rows, n), bf16),)
        own, *sends = call(
            functools.partial(stage_kernel, radix, place),
            outs, own, *got,
            scratch=[pltpu.VMEM((rows, n), f32)],
        )
        rows = small
    for at, (shift, radix) in reversed(list(enumerate(stages))):
        got = [flipped(own, k << shift) for k in range(1, radix)]
        if at:
            outs = (((rows * radix, n), bf16),)
            join = functools.partial(join_kernel, (shift, radix))
            (own,) = call(join, outs, own, *got)
            rows = rows * radix
    return (own, *got)


def probe_step(rate, probe, pieces):
    place = digits(lax.axis_size("tile"))[0]
    chunks = probe.reshape(place[1], -1, probe.shape[-1])
    (out,) = call(
        functools.partial(apply_kernel, rate, place),
        ((chunks.shape, f32),), chunks, *pieces,
    )
    return out.reshape(probe.shape)


def steps(obj, probe, mode_weights, measured, corner, counts, weight_index):
    n = probe.shape[-1]
    t = obj.shape[-1]
    one, two = dft_tables(n)
    rate = step_probe / (POS_DEV * lax.axis_size("tile"))
    state, half, rest, *edges = enter(obj[0], n)
    pm = probe
    po = swapped(probe)
    wm = mode_weights.T
    wo = swapped(wm)
    spots = corner.T
    for sweep in range(ITERS):
        low = shifted(edges[1], -GC)
        diag = shifted(edges[2], -(GC + 1))
        right = shifted(edges[0], -1)
        mine = (half, right, low, diag)
        other = (rest, swapped(right), swapped(low), swapped(diag))
        own_keep, own_send, edge_keep, edge_send, pgm, pgo = patches(
            counts, spots, weight_index, wm, wo, mine, other, measured, pm, po, one, two
        )
        edge_got = swapped(edge_send)
        right, low, diag = margins(edge_keep, edge_got, t, n)
        low = shifted(low, GC)
        diag = shifted(diag, GC + 1)
        right = shifted(right, 1)
        pieces = probe_sum(pgm, swapped(pgo))
        own_got = swapped(own_send)
        state, half, *edges = update(state, own_keep, own_got, right, low, diag)
        pm = probe_step(rate, pm, pieces)
        if sweep < ITERS - 1:
            rest = swapped(half)
            others = [swapped(piece) for piece in pieces]
            po = probe_step(rate, po, others)
    return (leave(state, swapped(state))[None], pm)


def solution(mesh):
    placed = (
        P("tile", None, None, None),
        P("mode", None, None, None),
        P(None, "mode"),
        P("tile", None, None),
        P("tile", None),
        P("tile"),
        P("tile"),
    )
    return jax.shard_map(
        steps,
        mesh=mesh,
        in_specs=placed,
        out_specs=(P("tile", None, None, None), P("mode", None, None, None)),
        check_vma=False,
    )
```

```python
import functools
import math

import jax
import jax.numpy as jnp
from jax import lax
from jax.experimental import pallas as pl
from jax.experimental.pallas import tpu as pltpu
from jax.sharding import PartitionSpec as P


GC = 8
POS_DEV = 2
ITERS = 2
STRIP = 32

step_object = 0.1
step_probe = 4.0

f32 = jnp.float32
bf16 = jnp.bfloat16
VM = pl.BlockSpec(memory_space=pltpu.VMEM)
SM = pl.BlockSpec(memory_space=pltpu.SMEM)


def shifted(array, by):
    peers = lax.axis_size("tile")
    return lax.ppermute(array, "tile", [(i, (i + by) % peers) for i in range(peers)])


def flipped(array, mask):
    peers = lax.axis_size("tile")
    return lax.ppermute(array, "tile", [(i, i ^ mask) for i in range(peers)])


def swapped(array):
    return lax.ppermute(array, "mode", [(0, 1), (1, 0)])


def dft_tables(length):
    half = jnp.arange(length // 2, dtype=jnp.int32)
    factor = 1.0 / math.sqrt(length)
    tall, wide = [], []
    for parity in (0, 1):
        product = (2 * half[:, None] + parity) * half[None, :] % length
        for value, out in ((product, tall), (product.T, wide)):
            angle = value.astype(f32) * (2.0 * math.pi / length)
            real = jnp.cos(angle) * factor
            imag = -(jnp.sin(angle) * factor)
            if out is tall:
                rows = [[real, -imag], [imag, real]]
            else:
                rows = [[real, imag], [-imag, real]]
            out.append(jnp.concatenate([jnp.concatenate(row, 1) for row in rows], 0))
    return jnp.stack(tall).astype(bf16), jnp.stack(wide).astype(bf16)


def dot(a, b):
    return jnp.dot(a, b, preferred_element_type=f32)


LANES = 128


def blocks(t, n, refs):
    right, low, diag = refs
    return ((right, 0, t, t, n), (low, t, 0, n, t), (diag, t, t, n, n))


def packed_rows(t, n):
    return (t * n // LANES, n * t // LANES, n * n // LANES)


def patch_kernel(
    live, corner, kind, wm, wo,
    tm, rm, bm, dm, to, ro, bo, do, meas, pm, po, tall, wide_table,
    own_keep, own_send, edge_keep, edge_send, pgm, pgo,
    frame, grad, psi, xs, ts, orr, oii, term, acc,
):
    n = pm.shape[-1]
    t = tm.shape[-1]
    half = pm.shape[0]
    modes = 2 * half
    me = lax.axis_index("mode")
    h = n // 2
    for plane, (a, b, c, d) in ((me, (tm, rm, bm, dm)), (1 - me, (to, ro, bo, do))):
        frame[plane, pl.ds(0, t), pl.ds(0, t)] = a[...].astype(f32)
        for ref, top, left, high, wide in blocks(t, n, (b, c, d)):
            for k in range(wide // LANES):
                part = ref[pl.ds(k * high, high), :].astype(f32)
                frame[plane, pl.ds(top, high), pl.ds(left + k * LANES, LANES)] = part
    grad[...] = jnp.zeros_like(grad)
    acc[...] = jnp.zeros_like(acc)
    term[...] = jnp.zeros_like(term)

    def probe_at(m, c, rows, cols=slice(None)):
        ref = pm if m < half else po
        return ref[m % half, c, rows, cols]

    def slot_body(g, carry):
        s = me + 2 * g

        @pl.when(s < live[0])
        def _():
            row = corner[0, s]
            col = corner[1, s]
            rb = pl.multiple_of(row // 8 * 8, 8)
            rr = row - rb
            cb = pl.multiple_of(col // 128 * 128, 128)
            cc = col - cb
            high, wide = n + 8, n + 128
            for p, out in ((0, orr), (1, oii)):
                win = frame[p, pl.ds(rb, high), pl.ds(cb, wide)]
                win = pltpu.roll(win, lax.rem(wide - cc, wide), 1)[:, :n]
                win = pltpu.roll(win, lax.rem(high - rr, high), 0)[:n]
                out[...] = win
            lanes = [pl.ds(q * h, h) for q in range(2)]
            w = [wm[m, kind[s]] if m < half else wo[m - half, kind[s]] for m in range(modes)]
            for m in range(modes):
                for i in range(h // STRIP):
                    up, low = pl.ds(i * STRIP, STRIP), pl.ds(h + i * STRIP, STRIP)
                    parts = []
                    for rows in (up, low):
                        a, b = orr[rows, :], oii[rows, :]
                        pr, pi = probe_at(m, 0, rows), probe_at(m, 1, rows)
                        parts.append((pr * a - pi * b, pr * b + pi * a))
                    (r0, i0), (r1, i1) = parts
                    xs[m, 0, up, :] = (r0 + r1).astype(bf16)
                    xs[m, 0, low, :] = (i0 + i1).astype(bf16)
                    xs[m, 1, up, :] = (r0 - r1).astype(bf16)
                    xs[m, 1, low, :] = (i0 - i1).astype(bf16)
            for m in range(modes):
                for p in range(2):
                    y = dot(tall[p], xs[m, p])
                    rows = pl.ds(m * n + p * h, h)
                    for c in range(2):
                        part = y[c * h : (c + 1) * h]
                        ts[0, rows, lanes[c]] = (part[:, :h] + part[:, h:]).astype(bf16)
                        ts[1, rows, lanes[c]] = (part[:, :h] - part[:, h:]).astype(bf16)
            for q in range(2):
                psi[q] = dot(ts[q], wide_table[q])
            for i in range(n // STRIP):
                p, base = divmod(i * STRIP, h)
                for q in range(2):
                    total = jnp.zeros((STRIP, h), f32)
                    for m in range(modes):
                        rows = pl.ds(m * n + i * STRIP, STRIP)
                        a, b = psi[q, rows, lanes[0]], psi[q, rows, lanes[1]]
                        total = total + w[m] * (a * a + b * b)
                    resid = total - meas[g, pl.ds(i * STRIP, STRIP), lanes[q]]
                    for m in range(modes):
                        rows = pl.ds(m * n + i * STRIP, STRIP)
                        scale = w[m] * resid
                        for c in range(2):
                            value = scale * psi[q, rows, lanes[c]]
                            xs[m, p, pl.ds(c * h + base, STRIP), lanes[q]] = value.astype(bf16)
            for m in range(modes):
                even = dot(wide_table[0], xs[m, 0])
                odd = dot(wide_table[1], xs[m, 1])
                for side, y in enumerate((even + odd, even - odd)):
                    rows = pl.ds(m * n + side * h, h)
                    for c in range(2):
                        part = y[c * h : (c + 1) * h].astype(bf16)
                        ts[0, rows, lanes[c]] = part[:, :h]
                        ts[1, rows, lanes[c]] = part[:, h:]
            for q in range(2):
                psi[q] = dot(ts[q], tall[q])
            for i in range(n // STRIP):
                up = pl.ds(i * STRIP, STRIP)
                for side in range(2):
                    cols = lanes[side]
                    a, b = orr[up, cols], oii[up, cols]
                    tr = jnp.zeros((STRIP, h), f32)
                    ti = jnp.zeros((STRIP, h), f32)
                    for m in range(modes):
                        rows = pl.ds(m * n + i * STRIP, STRIP)
                        sums = []
                        for c in range(2):
                            first, second = psi[0, rows, lanes[c]], psi[1, rows, lanes[c]]
                            sums.append(first - second if side else first + second)
                        cr, ci = sums
                        pr, pi = probe_at(m, 0, up, cols), probe_at(m, 1, up, cols)
                        tr = tr + (pr * cr + pi * ci)
                        ti = ti + (pr * ci - pi * cr)
                        acc[m, 0, up, cols] += a * cr + b * ci
                        acc[m, 1, up, cols] += a * ci - b * cr
                    term[0, up, cols] = tr
                    term[1, up, cols] = ti
            for p in range(2):
                moved = pltpu.roll(pltpu.roll(term[p], rr, 0), cc, 1)
                grad[p, pl.ds(rb, high), pl.ds(cb, wide)] += moved

        return carry

    lax.fori_loop(0, meas.shape[0], slot_body, 0)
    own_keep[...] = grad[me, pl.ds(0, t), pl.ds(0, t)]
    own_send[...] = grad[1 - me, pl.ds(0, t), pl.ds(0, t)].astype(bf16)
    base = 0
    for _, top, left, high, wide in blocks(t, n, (None,) * 3):
        for k in range(wide // LANES):
            rows, lanes = pl.ds(top, high), pl.ds(left + k * LANES, LANES)
            edge_keep[pl.ds(base, high), :] = grad[me, rows, lanes]
            edge_send[pl.ds(base, high), :] = grad[1 - me, rows, lanes].astype(bf16)
            base += high
    for m in range(half):
        pgm[m] = acc[m]
        pgo[m] = acc[half + m].astype(bf16)


def call(kernel, outs, *args, smem=0, scratch=(), limit=4 * 1024 * 1024):
    return pl.pallas_call(
        kernel,
        out_shape=tuple(jax.ShapeDtypeStruct(shape, dtype) for shape, dtype in outs),
        in_specs=[SM] * smem + [VM] * (len(args) - smem),
        out_specs=(VM,) * len(outs),
        scratch_shapes=list(scratch),
        compiler_params=pltpu.CompilerParams(vmem_limit_bytes=limit),
        name="kernel",
    )(*args)


def sort_kernel(meas, out):
    me = lax.axis_index("mode")
    n = out.shape[-1]
    h = n // 2
    row = lax.broadcasted_iota(jnp.int32, (n, n), 0)
    col = lax.broadcasted_iota(jnp.int32, (n, n), 1)

    def source(i):
        return jnp.where(i < h, 2 * i, 2 * i - (n - 1))

    def exact(product, value):
        total = jnp.zeros_like(value)
        for _ in range(3):
            part = value.astype(bf16)
            total = total + product(part)
            value = value - part.astype(f32)
        return total

    right = (row == source(col)).astype(f32).astype(bf16)
    left = (col == source(row)).astype(f32).astype(bf16)
    for g in range(out.shape[0]):
        value = exact(lambda part: dot(part, right), meas[me + 2 * g])
        out[g] = exact(lambda part: dot(left, part), value)


def sort(meas):
    outs = (((meas.shape[0] // 2, *meas.shape[1:]), f32),)
    return call(sort_kernel, outs, meas)[0]


def patches(live, corner, kind, wm, wo, mine, other, meas, pm, po, tall, wide):
    n = pm.shape[-1]
    t = mine[0].shape[-1]
    f = n + t
    modes = 2 * pm.shape[0]
    rows = sum(packed_rows(t, n))
    return call(
        patch_kernel,
        (
            ((t, t), f32),
            ((t, t), bf16),
            ((rows, LANES), f32),
            ((rows, LANES), bf16),
            (pm.shape, f32),
            (pm.shape, bf16),
        ),
        live, corner, kind, wm, wo, *mine, *other, meas, pm, po, tall, wide,
        smem=5,
        scratch=[
            pltpu.VMEM((2, f, f), f32),
            pltpu.VMEM((2, f, f), f32),
            pltpu.VMEM((2, modes * n, n), f32),
            pltpu.VMEM((modes, 2, n, n), bf16),
            pltpu.VMEM((2, modes * n, n), bf16),
            pltpu.VMEM((n, n), f32),
            pltpu.VMEM((n, n), f32),
            pltpu.VMEM((2, n + 8, n + 128), f32),
            pltpu.VMEM((modes, 2, n, n), f32),
        ],
        limit=24 * 1024 * 1024,
    )


def pack_edges(value, t, n, outs):
    for out, _, _, high, wide in blocks(t, n, outs):
        for k in range(wide // LANES):
            out[pl.ds(k * high, high), :] = value[:high, k * LANES : (k + 1) * LANES]


def enter_kernel(obj, state, half, rest, hr, hl, hd):
    me = lax.axis_index("mode")
    t = obj.shape[-1]
    n = hl.shape[0] * LANES // t
    value = obj[me]
    state[...] = value
    small = value.astype(bf16)
    half[...] = small
    pack_edges(small, t, n, (hr, hl, hd))
    rest[...] = obj[1 - me].astype(bf16)


def edge_shapes(t, n):
    return tuple(((rows, LANES), bf16) for rows in packed_rows(t, n))


def enter(obj, n):
    t = obj.shape[-1]
    outs = (((t, t), f32), ((t, t), bf16), ((t, t), bf16)) + edge_shapes(t, n)
    return call(enter_kernel, outs, obj)


def margin_kernel(keep, got, right, low, diag):
    base = 0
    for out in (right, low, diag):
        rows = pl.ds(base, out.shape[0])
        out[...] = (keep[rows, :] + got[rows, :].astype(f32)).astype(bf16)
        base += out.shape[0]


def margins(keep, got, t, n):
    return call(margin_kernel, edge_shapes(t, n), keep, got)


def update_kernel(state, keep, got, right, low, diag, new, half, hr, hl, hd):
    t = state.shape[0]
    n = low.shape[0] * LANES // t
    new[...] = keep[...] + got[...].astype(f32)
    for ref, _, _, high, wide in blocks(t, n, (right, low, diag)):
        for k in range(wide // LANES):
            lanes = pl.ds(k * LANES, LANES)
            new[pl.ds(0, high), lanes] += ref[pl.ds(k * high, high), :].astype(f32)
    value = state[...] - step_object * new[...]
    new[...] = value
    small = value.astype(bf16)
    half[...] = small
    pack_edges(small, t, n, (hr, hl, hd))


def update(state, keep, got, right, low, diag):
    t = state.shape[0]
    n = low.shape[0] * LANES // t
    outs = (((t, t), f32), ((t, t), bf16)) + edge_shapes(t, n)
    return call(update_kernel, outs, state, keep, got, right, low, diag)


def leave_kernel(state, rest, out):
    me = lax.axis_index("mode")
    out[me] = state[...]
    out[1 - me] = rest[...]


def leave(state, rest):
    outs = (((2, *state.shape), f32),)
    return call(leave_kernel, outs, state, rest)[0]


def digits(peers):
    out, shift = [], 0
    while 1 << shift < peers:
        radix = 4 if (4 << shift) <= peers else 2
        out.append((shift, radix))
        shift += radix.bit_length() - 1
    return out


def spot_of(shift, radix):
    return (lax.axis_index("tile") >> shift) & (radix - 1)


def first_kernel(place, keep, got, own, *sends):
    i = spot_of(*place)
    own[...] = keep[i] + got[i].astype(f32)
    for k, out in enumerate(sends):
        j = i ^ (k + 1)
        out[...] = (keep[j] + got[j].astype(f32)).astype(bf16)


def stage_kernel(before, place, have, *refs):
    after = place[1]
    got = refs[: before - 1]
    own, sends = refs[before - 1], refs[before:]
    total = refs[-1]
    sends = sends[:-1]
    value = have[...]
    for ref in got:
        value = value + ref[...].astype(f32)
    if after == 1:
        own[...] = value.astype(bf16)
        return
    total[...] = value
    rows = own.shape[0]
    i = spot_of(*place)
    own[...] = total[pl.ds(pl.multiple_of(i * rows, rows), rows), :]
    for k, out in enumerate(sends):
        j = i ^ (k + 1)
        out[...] = total[pl.ds(pl.multiple_of(j * rows, rows), rows), :].astype(bf16)


def join_kernel(place, have, *refs):
    got, out = refs[:-1], refs[-1]
    rows = have.shape[0]
    i = spot_of(*place)
    out[pl.ds(pl.multiple_of(i * rows, rows), rows), :] = have[...]
    for k, ref in enumerate(got):
        j = i ^ (k + 1)
        out[pl.ds(pl.multiple_of(j * rows, rows), rows), :] = ref[...]


def apply_kernel(rate, place, probe, have, *refs):
    got, out = refs[:-1], refs[-1]
    i = spot_of(*place)
    for k, ref in enumerate((have, *got)):
        j = i ^ k
        out[j] = probe[j] - rate * ref[...].astype(f32)


def probe_sum(keep, got):
    n = keep.shape[-1]
    stages = digits(lax.axis_size("tile"))
    shift, radix = stages[0]
    keep = keep.reshape(radix, -1, n)
    got = got.reshape(keep.shape)
    rows = keep.shape[1]
    own, *sends = call(
        functools.partial(first_kernel, (shift, radix)),
        (((rows, n), f32),) + (((rows, n), bf16),) * (radix - 1),
        keep, got,
    )
    for at, (shift, radix) in enumerate(stages):
        got = [flipped(part, (k + 1) << shift) for k, part in enumerate(sends)]
        if at + 1 < len(stages):
            place = stages[at + 1]
            small = rows // place[1]
            outs = (((small, n), f32),) + (((small, n), bf16),) * (place[1] - 1)
        else:
            place, small = (0, 1), rows
            outs = (((rows, n), bf16),)
        own, *sends = call(
            functools.partial(stage_kernel, radix, place),
            outs, own, *got,
            scratch=[pltpu.VMEM((rows, n), f32)],
        )
        rows = small
    for at, (shift, radix) in reversed(list(enumerate(stages))):
        got = [flipped(own, k << shift) for k in range(1, radix)]
        if at:
            outs = (((rows * radix, n), bf16),)
            join = functools.partial(join_kernel, (shift, radix))
            (own,) = call(join, outs, own, *got)
            rows = rows * radix
    return (own, *got)


def probe_step(rate, probe, pieces):
    place = digits(lax.axis_size("tile"))[0]
    chunks = probe.reshape(place[1], -1, probe.shape[-1])
    (out,) = call(
        functools.partial(apply_kernel, rate, place),
        ((chunks.shape, f32),), chunks, *pieces,
    )
    return out.reshape(probe.shape)


def steps(obj, probe, mode_weights, measured, corner, counts, weight_index):
    n = probe.shape[-1]
    t = obj.shape[-1]
    tall, wide = dft_tables(n)
    rate = step_probe / (POS_DEV * lax.axis_size("tile"))
    state, half, rest, *edges = enter(obj[0], n)
    pm = probe
    po = swapped(probe)
    wm = mode_weights.T
    wo = swapped(wm)
    spots = corner.T
    meas = sort(measured)
    for sweep in range(ITERS):
        low = shifted(edges[1], -GC)
        diag = shifted(edges[2], -(GC + 1))
        right = shifted(edges[0], -1)
        mine = (half, right, low, diag)
        other = (rest, swapped(right), swapped(low), swapped(diag))
        own_keep, own_send, edge_keep, edge_send, pgm, pgo = patches(
            counts, spots, weight_index, wm, wo, mine, other, meas, pm, po, tall, wide
        )
        edge_got = swapped(edge_send)
        right, low, diag = margins(edge_keep, edge_got, t, n)
        low = shifted(low, GC)
        diag = shifted(diag, GC + 1)
        right = shifted(right, 1)
        pieces = probe_sum(pgm, swapped(pgo))
        own_got = swapped(own_send)
        state, half, *edges = update(state, own_keep, own_got, right, low, diag)
        pm = probe_step(rate, pm, pieces)
        if sweep < ITERS - 1:
            rest = swapped(half)
            others = [swapped(piece) for piece in pieces]
            po = probe_step(rate, po, others)
    return (leave(state, swapped(state))[None], pm)


def solution(mesh):
    placed = (
        P("tile", None, None, None),
        P("mode", None, None, None),
        P(None, "mode"),
        P("tile", None, None),
        P("tile", None),
        P("tile"),
        P("tile"),
    )
    return jax.shard_map(
        steps,
        mesh=mesh,
        in_specs=placed,
        out_specs=(P("tile", None, None, None), P("mode", None, None, None)),
        check_vma=False,
    )
```

```python
import functools
import math

import jax
import jax.numpy as jnp
from jax import lax
from jax.experimental import pallas as pl
from jax.experimental.pallas import tpu as pltpu
from jax.sharding import PartitionSpec as P


GC = 8
POS_DEV = 2
ITERS = 2
STRIP = 32

step_object = 0.1
step_probe = 4.0

f32 = jnp.float32
bf16 = jnp.bfloat16
VM = pl.BlockSpec(memory_space=pltpu.VMEM)
SM = pl.BlockSpec(memory_space=pltpu.SMEM)


def shifted(array, by):
    peers = lax.axis_size("tile")
    return lax.ppermute(array, "tile", [(i, (i + by) % peers) for i in range(peers)])


def flipped(array, mask):
    peers = lax.axis_size("tile")
    return lax.ppermute(array, "tile", [(i, i ^ mask) for i in range(peers)])


def swapped(array):
    return lax.ppermute(array, "mode", [(0, 1), (1, 0)])


def dft_tables(length):
    half = jnp.arange(length // 2, dtype=jnp.int32)
    factor = 1.0 / math.sqrt(length)
    tall, wide = [], []
    for parity in (0, 1):
        product = (2 * half[:, None] + parity) * half[None, :] % length
        for value, out in ((product, tall), (product.T, wide)):
            angle = value.astype(f32) * (2.0 * math.pi / length)
            real = jnp.cos(angle) * factor
            imag = -(jnp.sin(angle) * factor)
            if out is tall:
                rows = [[real, -imag], [imag, real]]
            else:
                rows = [[real, imag], [-imag, real]]
            out.append(jnp.concatenate([jnp.concatenate(row, 1) for row in rows], 0))
    return jnp.stack(tall).astype(bf16), jnp.stack(wide).astype(bf16)


def dot(a, b):
    return jnp.dot(a, b, preferred_element_type=f32)


LANES = 128


def blocks(t, n, refs):
    right, low, diag = refs
    return ((right, 0, t, t, n), (low, t, 0, n, t), (diag, t, t, n, n))


def packed_rows(t, n):
    return (t * n // LANES, n * t // LANES, n * n // LANES)


def patch_kernel(
    live, corner, kind, wm, wo,
    tm, rm, bm, dm, to, ro, bo, do, meas, pm, po, tall, wide_table,
    own_keep, own_send, edge_keep, edge_send, pgm, pgo,
    frame, grad, psi, xs, ts, orr, oii, term, acc,
):
    n = pm.shape[-1]
    t = tm.shape[-1]
    half = pm.shape[0]
    modes = 2 * half
    me = lax.axis_index("mode")
    h = n // 2
    for plane, (a, b, c, d) in ((me, (tm, rm, bm, dm)), (1 - me, (to, ro, bo, do))):
        frame[plane, pl.ds(0, t), pl.ds(0, t)] = a[...].astype(f32)
        for ref, top, left, high, wide in blocks(t, n, (b, c, d)):
            for k in range(wide // LANES):
                part = ref[pl.ds(k * high, high), :].astype(f32)
                frame[plane, pl.ds(top, high), pl.ds(left + k * LANES, LANES)] = part
    grad[...] = jnp.zeros_like(grad)
    acc[...] = jnp.zeros_like(acc)
    term[...] = jnp.zeros_like(term)

    def probe_at(m, c, rows, cols=slice(None)):
        ref = pm if m < half else po
        return ref[m % half, c, rows, cols]

    def slot_body(g, carry):
        s = me + 2 * g

        @pl.when(s < live[0])
        def _():
            row = corner[0, s]
            col = corner[1, s]
            rb = pl.multiple_of(row // 8 * 8, 8)
            rr = row - rb
            cb = pl.multiple_of(col // 128 * 128, 128)
            cc = col - cb
            high, wide = n + 8, n + 128
            for p, out in ((0, orr), (1, oii)):
                win = frame[p, pl.ds(rb, high), pl.ds(cb, wide)]
                win = pltpu.roll(win, lax.rem(wide - cc, wide), 1)[:, :n]
                win = pltpu.roll(win, lax.rem(high - rr, high), 0)[:n]
                out[...] = win
            lanes = [pl.ds(q * h, h) for q in range(2)]
            w = [wm[m, kind[s]] if m < half else wo[m - half, kind[s]] for m in range(modes)]
            for m in range(modes):
                for i in range(h // STRIP):
                    up, low = pl.ds(i * STRIP, STRIP), pl.ds(h + i * STRIP, STRIP)
                    parts = []
                    for rows in (up, low):
                        a, b = orr[rows, :], oii[rows, :]
                        pr, pi = probe_at(m, 0, rows), probe_at(m, 1, rows)
                        parts.append((pr * a - pi * b, pr * b + pi * a))
                    (r0, i0), (r1, i1) = parts
                    xs[m, 0, up, :] = (r0 + r1).astype(bf16)
                    xs[m, 0, low, :] = (i0 + i1).astype(bf16)
                    xs[m, 1, up, :] = (r0 - r1).astype(bf16)
                    xs[m, 1, low, :] = (i0 - i1).astype(bf16)
            for m in range(modes):
                for p in range(2):
                    y = dot(tall[p], xs[m, p])
                    rows = pl.ds(m * n + p * h, h)
                    for c in range(2):
                        part = y[c * h : (c + 1) * h]
                        ts[0, rows, lanes[c]] = (part[:, :h] + part[:, h:]).astype(bf16)
                        ts[1, rows, lanes[c]] = (part[:, :h] - part[:, h:]).astype(bf16)
            for q in range(2):
                psi[q] = dot(ts[q], wide_table[q])
            for i in range(n // STRIP):
                p, base = divmod(i * STRIP, h)
                for q in range(2):
                    total = jnp.zeros((STRIP, h), f32)
                    for m in range(modes):
                        rows = pl.ds(m * n + i * STRIP, STRIP)
                        a, b = psi[q, rows, lanes[0]], psi[q, rows, lanes[1]]
                        total = total + w[m] * (a * a + b * b)
                    resid = total - meas[g, pl.ds(i * STRIP, STRIP), lanes[q]]
                    for m in range(modes):
                        rows = pl.ds(m * n + i * STRIP, STRIP)
                        scale = w[m] * resid
                        for c in range(2):
                            value = scale * psi[q, rows, lanes[c]]
                            xs[m, p, pl.ds(c * h + base, STRIP), lanes[q]] = value.astype(bf16)
            for m in range(modes):
                even = dot(wide_table[0], xs[m, 0])
                odd = dot(wide_table[1], xs[m, 1])
                for side, y in enumerate((even + odd, even - odd)):
                    rows = pl.ds(m * n + side * h, h)
                    for c in range(2):
                        part = y[c * h : (c + 1) * h].astype(bf16)
                        ts[0, rows, lanes[c]] = part[:, :h]
                        ts[1, rows, lanes[c]] = part[:, h:]
            for q in range(2):
                psi[q] = dot(ts[q], tall[q])
            for i in range(n // STRIP):
                up = pl.ds(i * STRIP, STRIP)
                for side in range(2):
                    cols = lanes[side]
                    a, b = orr[up, cols], oii[up, cols]
                    tr = jnp.zeros((STRIP, h), f32)
                    ti = jnp.zeros((STRIP, h), f32)
                    for m in range(modes):
                        rows = pl.ds(m * n + i * STRIP, STRIP)
                        sums = []
                        for c in range(2):
                            first, second = psi[0, rows, lanes[c]], psi[1, rows, lanes[c]]
                            sums.append(first - second if side else first + second)
                        cr, ci = sums
                        pr, pi = probe_at(m, 0, up, cols), probe_at(m, 1, up, cols)
                        tr = tr + (pr * cr + pi * ci)
                        ti = ti + (pr * ci - pi * cr)
                        acc[m, 0, up, cols] += a * cr + b * ci
                        acc[m, 1, up, cols] += a * ci - b * cr
                    term[0, up, cols] = tr
                    term[1, up, cols] = ti
            for p in range(2):
                moved = pltpu.roll(pltpu.roll(term[p], rr, 0), cc, 1)
                grad[p, pl.ds(rb, high), pl.ds(cb, wide)] += moved

        return carry

    lax.fori_loop(0, meas.shape[0], slot_body, 0)
    own_keep[...] = grad[me, pl.ds(0, t), pl.ds(0, t)]
    own_send[...] = grad[1 - me, pl.ds(0, t), pl.ds(0, t)].astype(bf16)
    base = 0
    for _, top, left, high, wide in blocks(t, n, (None,) * 3):
        for k in range(wide // LANES):
            rows, lanes = pl.ds(top, high), pl.ds(left + k * LANES, LANES)
            edge_keep[pl.ds(base, high), :] = grad[me, rows, lanes]
            edge_send[pl.ds(base, high), :] = grad[1 - me, rows, lanes].astype(bf16)
            base += high
    for m in range(half):
        pgm[m] = acc[m]
        pgo[m] = acc[half + m].astype(bf16)


def call(kernel, outs, *args, smem=0, scratch=(), limit=4 * 1024 * 1024):
    return pl.pallas_call(
        kernel,
        out_shape=tuple(jax.ShapeDtypeStruct(shape, dtype) for shape, dtype in outs),
        in_specs=[SM] * smem + [VM] * (len(args) - smem),
        out_specs=(VM,) * len(outs),
        scratch_shapes=list(scratch),
        compiler_params=pltpu.CompilerParams(vmem_limit_bytes=limit),
        name="kernel",
    )(*args)


def sort_kernel(meas, tall, wide, out):
    me = lax.axis_index("mode")
    n = out.shape[-1]
    h = n // 2
    row = lax.broadcasted_iota(jnp.int32, (n, n), 0)
    col = lax.broadcasted_iota(jnp.int32, (n, n), 1)

    def source(i):
        return jnp.where(i < h, 2 * i, 2 * i - (n - 1))

    def exact(product, value):
        total = jnp.zeros_like(value)
        for _ in range(3):
            part = value.astype(bf16)
            total = total + product(part)
            value = value - part.astype(f32)
        return total

    right = (row == source(col)).astype(f32).astype(bf16)
    left = (col == source(row)).astype(f32).astype(bf16)
    for g in range(out.shape[0]):
        value = exact(lambda part: dot(part, right), meas[me + 2 * g])
        out[g] = exact(lambda part: dot(left, part), value)


def sort(meas, tall, wide):
    outs = (((meas.shape[0] // 2, *meas.shape[1:]), f32),)
    return call(sort_kernel, outs, meas, tall, wide)[0]


def patches(live, corner, kind, wm, wo, mine, other, meas, pm, po, tall, wide):
    n = pm.shape[-1]
    t = mine[0].shape[-1]
    f = n + t
    modes = 2 * pm.shape[0]
    rows = sum(packed_rows(t, n))
    return call(
        patch_kernel,
        (
            ((t, t), f32),
            ((t, t), bf16),
            ((rows, LANES), f32),
            ((rows, LANES), bf16),
            (pm.shape, f32),
            (pm.shape, bf16),
        ),
        live, corner, kind, wm, wo, *mine, *other, meas, pm, po, tall, wide,
        smem=5,
        scratch=[
            pltpu.VMEM((2, f, f), f32),
            pltpu.VMEM((2, f, f), f32),
            pltpu.VMEM((2, modes * n, n), f32),
            pltpu.VMEM((modes, 2, n, n), bf16),
            pltpu.VMEM((2, modes * n, n), bf16),
            pltpu.VMEM((n, n), f32),
            pltpu.VMEM((n, n), f32),
            pltpu.VMEM((2, n + 8, n + 128), f32),
            pltpu.VMEM((modes, 2, n, n), f32),
        ],
        limit=24 * 1024 * 1024,
    )


def pack_edges(value, t, n, outs):
    for out, _, _, high, wide in blocks(t, n, outs):
        for k in range(wide // LANES):
            out[pl.ds(k * high, high), :] = value[:high, k * LANES : (k + 1) * LANES]


def enter_kernel(obj, state, half, rest, hr, hl, hd):
    me = lax.axis_index("mode")
    t = obj.shape[-1]
    n = hl.shape[0] * LANES // t
    value = obj[me]
    state[...] = value
    small = value.astype(bf16)
    half[...] = small
    pack_edges(small, t, n, (hr, hl, hd))
    rest[...] = obj[1 - me].astype(bf16)


def edge_shapes(t, n):
    return tuple(((rows, LANES), bf16) for rows in packed_rows(t, n))


def enter(obj, n):
    t = obj.shape[-1]
    outs = (((t, t), f32), ((t, t), bf16), ((t, t), bf16)) + edge_shapes(t, n)
    return call(enter_kernel, outs, obj)


def margin_kernel(keep, got, right, low, diag):
    base = 0
    for out in (right, low, diag):
        rows = pl.ds(base, out.shape[0])
        out[...] = (keep[rows, :] + got[rows, :].astype(f32)).astype(bf16)
        base += out.shape[0]


def margins(keep, got, t, n):
    return call(margin_kernel, edge_shapes(t, n), keep, got)


def update_kernel(state, keep, got, right, low, diag, new, half, hr, hl, hd):
    t = state.shape[0]
    n = low.shape[0] * LANES // t
    new[...] = keep[...] + got[...].astype(f32)
    for ref, _, _, high, wide in blocks(t, n, (right, low, diag)):
        for k in range(wide // LANES):
            lanes = pl.ds(k * LANES, LANES)
            new[pl.ds(0, high), lanes] += ref[pl.ds(k * high, high), :].astype(f32)
    value = state[...] - step_object * new[...]
    new[...] = value
    small = value.astype(bf16)
    half[...] = small
    pack_edges(small, t, n, (hr, hl, hd))


def update(state, keep, got, right, low, diag):
    t = state.shape[0]
    n = low.shape[0] * LANES // t
    outs = (((t, t), f32), ((t, t), bf16)) + edge_shapes(t, n)
    return call(update_kernel, outs, state, keep, got, right, low, diag)


def leave_kernel(state, rest, out):
    me = lax.axis_index("mode")
    out[me] = state[...]
    out[1 - me] = rest[...]


def leave(state, rest):
    outs = (((2, *state.shape), f32),)
    return call(leave_kernel, outs, state, rest)[0]


def digits(peers):
    out, shift = [], 0
    while 1 << shift < peers:
        radix = 4 if (4 << shift) <= peers else 2
        out.append((shift, radix))
        shift += radix.bit_length() - 1
    return out


def spot_of(shift, radix):
    return (lax.axis_index("tile") >> shift) & (radix - 1)


def first_kernel(place, keep, got, own, *sends):
    i = spot_of(*place)
    own[...] = keep[i] + got[i].astype(f32)
    for k, out in enumerate(sends):
        j = i ^ (k + 1)
        out[...] = (keep[j] + got[j].astype(f32)).astype(bf16)


def stage_kernel(before, place, have, *refs):
    after = place[1]
    got = refs[: before - 1]
    own, sends = refs[before - 1], refs[before:]
    total = refs[-1]
    sends = sends[:-1]
    value = have[...]
    for ref in got:
        value = value + ref[...].astype(f32)
    if after == 1:
        own[...] = value.astype(bf16)
        return
    total[...] = value
    rows = own.shape[0]
    i = spot_of(*place)
    own[...] = total[pl.ds(pl.multiple_of(i * rows, rows), rows), :]
    for k, out in enumerate(sends):
        j = i ^ (k + 1)
        out[...] = total[pl.ds(pl.multiple_of(j * rows, rows), rows), :].astype(bf16)


def join_kernel(place, have, *refs):
    got, out = refs[:-1], refs[-1]
    rows = have.shape[0]
    i = spot_of(*place)
    out[pl.ds(pl.multiple_of(i * rows, rows), rows), :] = have[...]
    for k, ref in enumerate(got):
        j = i ^ (k + 1)
        out[pl.ds(pl.multiple_of(j * rows, rows), rows), :] = ref[...]


def apply_kernel(rate, place, probe, have, *refs):
    got, out = refs[:-1], refs[-1]
    i = spot_of(*place)
    for k, ref in enumerate((have, *got)):
        j = i ^ k
        out[j] = probe[j] - rate * ref[...].astype(f32)


def probe_sum(keep, got):
    n = keep.shape[-1]
    stages = digits(lax.axis_size("tile"))
    shift, radix = stages[0]
    keep = keep.reshape(radix, -1, n)
    got = got.reshape(keep.shape)
    rows = keep.shape[1]
    own, *sends = call(
        functools.partial(first_kernel, (shift, radix)),
        (((rows, n), f32),) + (((rows, n), bf16),) * (radix - 1),
        keep, got,
    )
    for at, (shift, radix) in enumerate(stages):
        got = [flipped(part, (k + 1) << shift) for k, part in enumerate(sends)]
        if at + 1 < len(stages):
            place = stages[at + 1]
            small = rows // place[1]
            outs = (((small, n), f32),) + (((small, n), bf16),) * (place[1] - 1)
        else:
            place, small = (0, 1), rows
            outs = (((rows, n), bf16),)
        own, *sends = call(
            functools.partial(stage_kernel, radix, place),
            outs, own, *got,
            scratch=[pltpu.VMEM((rows, n), f32)],
        )
        rows = small
    for at, (shift, radix) in reversed(list(enumerate(stages))):
        got = [flipped(own, k << shift) for k in range(1, radix)]
        if at:
            outs = (((rows * radix, n), bf16),)
            join = functools.partial(join_kernel, (shift, radix))
            (own,) = call(join, outs, own, *got)
            rows = rows * radix
    return (own, *got)


def probe_step(rate, probe, pieces):
    place = digits(lax.axis_size("tile"))[0]
    chunks = probe.reshape(place[1], -1, probe.shape[-1])
    (out,) = call(
        functools.partial(apply_kernel, rate, place),
        ((chunks.shape, f32),), chunks, *pieces,
    )
    return out.reshape(probe.shape)


def steps(obj, probe, mode_weights, measured, corner, counts, weight_index):
    n = probe.shape[-1]
    t = obj.shape[-1]
    tall, wide = dft_tables(n)
    rate = step_probe / (POS_DEV * lax.axis_size("tile"))
    state, half, rest, *edges = enter(obj[0], n)
    pm = probe
    po = swapped(probe)
    wm = mode_weights.T
    wo = swapped(wm)
    spots = corner.T
    meas = sort(measured, tall, wide)
    for sweep in range(ITERS):
        low = shifted(edges[1], -GC)
        diag = shifted(edges[2], -(GC + 1))
        right = shifted(edges[0], -1)
        mine = (half, right, low, diag)
        other = (rest, swapped(right), swapped(low), swapped(diag))
        own_keep, own_send, edge_keep, edge_send, pgm, pgo = patches(
            counts, spots, weight_index, wm, wo, mine, other, meas, pm, po, tall, wide
        )
        edge_got = swapped(edge_send)
        right, low, diag = margins(edge_keep, edge_got, t, n)
        low = shifted(low, GC)
        diag = shifted(diag, GC + 1)
        right = shifted(right, 1)
        pieces = probe_sum(pgm, swapped(pgo))
        own_got = swapped(own_send)
        state, half, *edges = update(state, own_keep, own_got, right, low, diag)
        pm = probe_step(rate, pm, pieces)
        if sweep < ITERS - 1:
            rest = swapped(half)
            others = [swapped(piece) for piece in pieces]
            po = probe_step(rate, po, others)
    return (leave(state, swapped(state))[None], pm)


def solution(mesh):
    placed = (
        P("tile", None, None, None),
        P("mode", None, None, None),
        P(None, "mode"),
        P("tile", None, None),
        P("tile", None),
        P("tile"),
        P("tile"),
    )
    return jax.shard_map(
        steps,
        mesh=mesh,
        in_specs=placed,
        out_specs=(P("tile", None, None, None), P("mode", None, None, None)),
        check_vma=False,
    )
```

```python
import functools
import math

import jax
import jax.numpy as jnp
from jax import lax
from jax.experimental import pallas as pl
from jax.experimental.pallas import tpu as pltpu
from jax.sharding import PartitionSpec as P


GC = 8
POS_DEV = 2
ITERS = 2
STRIP = 32

step_object = 0.1
step_probe = 4.0

f32 = jnp.float32
bf16 = jnp.bfloat16
VM = pl.BlockSpec(memory_space=pltpu.VMEM)
SM = pl.BlockSpec(memory_space=pltpu.SMEM)


def shifted(array, by):
    peers = lax.axis_size("tile")
    return lax.ppermute(array, "tile", [(i, (i + by) % peers) for i in range(peers)])


def flipped(array, mask):
    peers = lax.axis_size("tile")
    return lax.ppermute(array, "tile", [(i, i ^ mask) for i in range(peers)])


def swapped(array):
    return lax.ppermute(array, "mode", [(0, 1), (1, 0)])


def dft_tables(length):
    half = jnp.arange(length // 2, dtype=jnp.int32)
    factor = 1.0 / math.sqrt(length)
    tall, wide = [], []
    for parity in (0, 1):
        product = (2 * half[:, None] + parity) * half[None, :] % length
        for value, out in ((product, tall), (product.T, wide)):
            angle = value.astype(f32) * (2.0 * math.pi / length)
            real = jnp.cos(angle) * factor
            imag = -(jnp.sin(angle) * factor)
            if out is tall:
                rows = [[real, -imag], [imag, real]]
            else:
                rows = [[real, imag], [-imag, real]]
            out.append(jnp.concatenate([jnp.concatenate(row, 1) for row in rows], 0))
    return jnp.stack(tall).astype(bf16), jnp.stack(wide).astype(bf16)


def dot(a, b):
    return jnp.dot(a, b, preferred_element_type=f32)


LANES = 128
SUBS = 8


def blocks(t, n, refs):
    right, low, diag = refs
    return ((right, 0, t, t, n), (low, t, 0, n, t), (diag, t, t, n, n))


def packed_rows(t, n):
    return (t * n // LANES, n * t // LANES, n * n // LANES)


def patch_kernel(
    live, corner, kind, wm, wo,
    tm, rm, bm, dm, to, ro, bo, do, meas, pm, po, tall, wide_table,
    own_keep, own_send, edge_keep, edge_send, pgm, pgo,
    frame, grad, psi, xs, ts, orr, oii, term, acc,
):
    n = pm.shape[-1]
    t = tm.shape[-1]
    half = pm.shape[0]
    modes = 2 * half
    me = lax.axis_index("mode")
    h = n // 2
    for plane, (a, b, c, d) in ((me, (tm, rm, bm, dm)), (1 - me, (to, ro, bo, do))):
        frame[plane, pl.ds(0, t), pl.ds(0, t)] = a[...].astype(f32)
        for ref, top, left, high, wide in blocks(t, n, (b, c, d)):
            for k in range(wide // LANES):
                part = ref[pl.ds(k * high, high), :].astype(f32)
                frame[plane, pl.ds(top, high), pl.ds(left + k * LANES, LANES)] = part
    grad[...] = jnp.zeros_like(grad)
    acc[...] = jnp.zeros_like(acc)

    def probe_at(m, c, rows, cols=slice(None)):
        ref = pm if m < half else po
        return ref[m % half, c, rows, cols]

    def slot_body(g, carry):
        s = me + 2 * g

        @pl.when(s < live[0])
        def _():
            row = corner[0, s]
            col = corner[1, s]
            cb = pl.multiple_of(col // LANES * LANES, LANES)
            cc = col - cb
            rb = pl.multiple_of(row // SUBS * SUBS, SUBS)
            rr = row - rb
            count, tall_count = n // LANES, n // SUBS
            lane = lax.broadcasted_iota(jnp.int32, (1, SUBS, LANES), 2)
            sub = lax.broadcasted_iota(jnp.int32, (1, SUBS, LANES), 1)
            rows = pl.ds(rb, n + SUBS)
            left, above = lane < LANES - cc, sub < SUBS - rr
            for p, out in ((0, orr), (1, oii)):
                turned = []
                for k in range(count + 1):
                    block = frame[p, rows, pl.ds(cb + k * LANES, LANES)]
                    block = block.reshape(tall_count + 1, SUBS, LANES)
                    turned.append(pltpu.roll(block, lax.rem(LANES - cc, LANES), 2))
                for k in range(count):
                    block = jnp.where(left, turned[k], turned[k + 1])
                    block = pltpu.roll(block, lax.rem(SUBS - rr, SUBS), 1)
                    block = jnp.where(above, block[:-1], block[1:])
                    out[:, pl.ds(k * LANES, LANES)] = block.reshape(n, LANES)
            lanes = [pl.ds(q * h, h) for q in range(2)]
            w = [wm[m, kind[s]] if m < half else wo[m - half, kind[s]] for m in range(modes)]
            for m in range(modes):
                for i in range(h // STRIP):
                    up, low = pl.ds(i * STRIP, STRIP), pl.ds(h + i * STRIP, STRIP)
                    parts = []
                    for rows in (up, low):
                        a, b = orr[rows, :], oii[rows, :]
                        pr, pi = probe_at(m, 0, rows), probe_at(m, 1, rows)
                        parts.append((pr * a - pi * b, pr * b + pi * a))
                    (r0, i0), (r1, i1) = parts
                    xs[m, 0, up, :] = (r0 + r1).astype(bf16)
                    xs[m, 0, low, :] = (i0 + i1).astype(bf16)
                    xs[m, 1, up, :] = (r0 - r1).astype(bf16)
                    xs[m, 1, low, :] = (i0 - i1).astype(bf16)
            for m in range(modes):
                for p in range(2):
                    y = dot(tall[p], xs[m, p])
                    rows = pl.ds(m * n + p * h, h)
                    for c in range(2):
                        part = y[c * h : (c + 1) * h]
                        ts[0, rows, lanes[c]] = (part[:, :h] + part[:, h:]).astype(bf16)
                        ts[1, rows, lanes[c]] = (part[:, :h] - part[:, h:]).astype(bf16)
            for q in range(2):
                psi[q] = dot(ts[q], wide_table[q])
            for i in range(n // STRIP):
                p, base = divmod(i * STRIP, h)
                for q in range(2):
                    total = jnp.zeros((STRIP, h), f32)
                    for m in range(modes):
                        rows = pl.ds(m * n + i * STRIP, STRIP)
                        a, b = psi[q, rows, lanes[0]], psi[q, rows, lanes[1]]
                        total = total + w[m] * (a * a + b * b)
                    resid = total - meas[g, pl.ds(i * STRIP, STRIP), lanes[q]]
                    for m in range(modes):
                        rows = pl.ds(m * n + i * STRIP, STRIP)
                        scale = w[m] * resid
                        for c in range(2):
                            value = scale * psi[q, rows, lanes[c]]
                            xs[m, p, pl.ds(c * h + base, STRIP), lanes[q]] = value.astype(bf16)
            for m in range(modes):
                even = dot(wide_table[0], xs[m, 0])
                odd = dot(wide_table[1], xs[m, 1])
                for side, y in enumerate((even + odd, even - odd)):
                    rows = pl.ds(m * n + side * h, h)
                    for c in range(2):
                        part = y[c * h : (c + 1) * h].astype(bf16)
                        ts[0, rows, lanes[c]] = part[:, :h]
                        ts[1, rows, lanes[c]] = part[:, h:]
            for q in range(2):
                psi[q] = dot(ts[q], tall[q])
            for i in range(n // STRIP):
                up = pl.ds(i * STRIP, STRIP)
                for side in range(2):
                    cols = lanes[side]
                    a, b = orr[up, cols], oii[up, cols]
                    tr = jnp.zeros((STRIP, h), f32)
                    ti = jnp.zeros((STRIP, h), f32)
                    for m in range(modes):
                        rows = pl.ds(m * n + i * STRIP, STRIP)
                        sums = []
                        for c in range(2):
                            first, second = psi[0, rows, lanes[c]], psi[1, rows, lanes[c]]
                            sums.append(first - second if side else first + second)
                        cr, ci = sums
                        pr, pi = probe_at(m, 0, up, cols), probe_at(m, 1, up, cols)
                        tr = tr + (pr * cr + pi * ci)
                        ti = ti + (pr * ci - pi * cr)
                        acc[m, 0, up, cols] += a * cr + b * ci
                        acc[m, 1, up, cols] += a * ci - b * cr
                    term[0, up, cols] = tr
                    term[1, up, cols] = ti
            rows = pl.ds(rb, n + SUBS)
            begun, over = lane < cc, sub < rr
            for p in range(2):
                turned = []
                for k in range(count):
                    block = term[p, :, pl.ds(k * LANES, LANES)]
                    block = pltpu.roll(block.reshape(tall_count, SUBS, LANES), rr, 1)
                    edge = jnp.zeros((1, SUBS, LANES), f32)
                    before = jnp.concatenate([edge, block], 0)
                    after = jnp.concatenate([block, edge], 0)
                    turned.append(pltpu.roll(jnp.where(over, before, after), cc, 2))
                nothing = jnp.zeros_like(turned[0])
                for k in range(count + 1):
                    low = turned[k - 1] if k else nothing
                    high = turned[k] if k < count else nothing
                    cols = pl.ds(cb + k * LANES, LANES)
                    moved = jnp.where(begun, low, high)
                    grad[p, rows, cols] += moved.reshape(n + SUBS, LANES)

        return carry

    lax.fori_loop(0, meas.shape[0], slot_body, 0)
    own_keep[...] = grad[me, pl.ds(0, t), pl.ds(0, t)]
    own_send[...] = grad[1 - me, pl.ds(0, t), pl.ds(0, t)].astype(bf16)
    base = 0
    for _, top, left, high, wide in blocks(t, n, (None,) * 3):
        for k in range(wide // LANES):
            rows, lanes = pl.ds(top, high), pl.ds(left + k * LANES, LANES)
            edge_keep[pl.ds(base, high), :] = grad[me, rows, lanes]
            edge_send[pl.ds(base, high), :] = grad[1 - me, rows, lanes].astype(bf16)
            base += high
    for m in range(half):
        pgm[m] = acc[m]
        pgo[m] = acc[half + m].astype(bf16)


def call(kernel, outs, *args, smem=0, scratch=(), limit=4 * 1024 * 1024):
    return pl.pallas_call(
        kernel,
        out_shape=tuple(jax.ShapeDtypeStruct(shape, dtype) for shape, dtype in outs),
        in_specs=[SM] * smem + [VM] * (len(args) - smem),
        out_specs=(VM,) * len(outs),
        scratch_shapes=list(scratch),
        compiler_params=pltpu.CompilerParams(vmem_limit_bytes=limit),
        name="kernel",
    )(*args)


def sort_kernel(meas, tall, wide, out):
    me = lax.axis_index("mode")
    n = out.shape[-1]
    h = n // 2
    row = lax.broadcasted_iota(jnp.int32, (n, n), 0)
    col = lax.broadcasted_iota(jnp.int32, (n, n), 1)

    def source(i):
        return jnp.where(i < h, 2 * i, 2 * i - (n - 1))

    def exact(product, value):
        total = jnp.zeros_like(value)
        for _ in range(3):
            part = value.astype(bf16)
            total = total + product(part)
            value = value - part.astype(f32)
        return total

    right = (row == source(col)).astype(f32).astype(bf16)
    left = (col == source(row)).astype(f32).astype(bf16)
    for g in range(out.shape[0]):
        value = exact(lambda part: dot(part, right), meas[me + 2 * g])
        out[g] = exact(lambda part: dot(left, part), value)


def sort(meas, tall, wide):
    outs = (((meas.shape[0] // 2, *meas.shape[1:]), f32),)
    return call(sort_kernel, outs, meas, tall, wide)[0]


def patches(live, corner, kind, wm, wo, mine, other, meas, pm, po, tall, wide):
    n = pm.shape[-1]
    t = mine[0].shape[-1]
    f = n + t
    modes = 2 * pm.shape[0]
    rows = sum(packed_rows(t, n))
    return call(
        patch_kernel,
        (
            ((t, t), f32),
            ((t, t), bf16),
            ((rows, LANES), f32),
            ((rows, LANES), bf16),
            (pm.shape, f32),
            (pm.shape, bf16),
        ),
        live, corner, kind, wm, wo, *mine, *other, meas, pm, po, tall, wide,
        smem=5,
        scratch=[
            pltpu.VMEM((2, f, f), f32),
            pltpu.VMEM((2, f, f), f32),
            pltpu.VMEM((2, modes * n, n), f32),
            pltpu.VMEM((modes, 2, n, n), bf16),
            pltpu.VMEM((2, modes * n, n), bf16),
            pltpu.VMEM((n, n), f32),
            pltpu.VMEM((n, n), f32),
            pltpu.VMEM((2, n, n), f32),
            pltpu.VMEM((modes, 2, n, n), f32),
        ],
        limit=24 * 1024 * 1024,
    )


def pack_edges(value, t, n, outs):
    for out, _, _, high, wide in blocks(t, n, outs):
        for k in range(wide // LANES):
            out[pl.ds(k * high, high), :] = value[:high, k * LANES : (k + 1) * LANES]


def enter_kernel(obj, state, half, rest, hr, hl, hd):
    me = lax.axis_index("mode")
    t = obj.shape[-1]
    n = hl.shape[0] * LANES // t
    value = obj[me]
    state[...] = value
    small = value.astype(bf16)
    half[...] = small
    pack_edges(small, t, n, (hr, hl, hd))
    rest[...] = obj[1 - me].astype(bf16)


def edge_shapes(t, n):
    return tuple(((rows, LANES), bf16) for rows in packed_rows(t, n))


def enter(obj, n):
    t = obj.shape[-1]
    outs = (((t, t), f32), ((t, t), bf16), ((t, t), bf16)) + edge_shapes(t, n)
    return call(enter_kernel, outs, obj)


def margin_kernel(keep, got, right, low, diag):
    base = 0
    for out in (right, low, diag):
        rows = pl.ds(base, out.shape[0])
        out[...] = (keep[rows, :] + got[rows, :].astype(f32)).astype(bf16)
        base += out.shape[0]


def margins(keep, got, t, n):
    return call(margin_kernel, edge_shapes(t, n), keep, got)


def update_kernel(state, keep, got, right, low, diag, new, half, hr, hl, hd):
    t = state.shape[0]
    n = low.shape[0] * LANES // t
    new[...] = keep[...] + got[...].astype(f32)
    for ref, _, _, high, wide in blocks(t, n, (right, low, diag)):
        for k in range(wide // LANES):
            lanes = pl.ds(k * LANES, LANES)
            new[pl.ds(0, high), lanes] += ref[pl.ds(k * high, high), :].astype(f32)
    value = state[...] - step_object * new[...]
    new[...] = value
    small = value.astype(bf16)
    half[...] = small
    pack_edges(small, t, n, (hr, hl, hd))


def update(state, keep, got, right, low, diag):
    t = state.shape[0]
    n = low.shape[0] * LANES // t
    outs = (((t, t), f32), ((t, t), bf16)) + edge_shapes(t, n)
    return call(update_kernel, outs, state, keep, got, right, low, diag)


def leave_kernel(state, rest, out):
    me = lax.axis_index("mode")
    out[me] = state[...]
    out[1 - me] = rest[...]


def leave(state, rest):
    outs = (((2, *state.shape), f32),)
    return call(leave_kernel, outs, state, rest)[0]


def digits(peers):
    out, shift = [], 0
    while 1 << shift < peers:
        radix = 4 if shift == 0 and peers >= 4 else 2
        out.append((shift, radix))
        shift += radix.bit_length() - 1
    return out


def spot_of(shift, radix):
    return (lax.axis_index("tile") >> shift) & (radix - 1)


def first_kernel(place, keep, got, own, *sends):
    i = spot_of(*place)
    own[...] = keep[i] + got[i].astype(f32)
    for k, out in enumerate(sends):
        j = i ^ (k + 1)
        out[...] = (keep[j] + got[j].astype(f32)).astype(bf16)


def stage_kernel(before, place, have, *refs):
    after = place[1]
    got = refs[: before - 1]
    own, sends = refs[before - 1], refs[before:]
    total = refs[-1]
    sends = sends[:-1]
    value = have[...]
    for ref in got:
        value = value + ref[...].astype(f32)
    if after == 1:
        own[...] = value.astype(bf16)
        return
    total[...] = value
    rows = own.shape[0]
    i = spot_of(*place)
    own[...] = total[pl.ds(pl.multiple_of(i * rows, rows), rows), :]
    for k, out in enumerate(sends):
        j = i ^ (k + 1)
        out[...] = total[pl.ds(pl.multiple_of(j * rows, rows), rows), :].astype(bf16)


def join_kernel(place, have, *refs):
    got, out = refs[:-1], refs[-1]
    rows = have.shape[0]
    i = spot_of(*place)
    out[pl.ds(pl.multiple_of(i * rows, rows), rows), :] = have[...]
    for k, ref in enumerate(got):
        j = i ^ (k + 1)
        out[pl.ds(pl.multiple_of(j * rows, rows), rows), :] = ref[...]


def apply_kernel(rate, place, probe, have, *refs):
    got, out = refs[:-1], refs[-1]
    i = spot_of(*place)
    for k, ref in enumerate((have, *got)):
        j = i ^ k
        out[j] = probe[j] - rate * ref[...].astype(f32)


def probe_sum(keep, got):
    n = keep.shape[-1]
    stages = digits(lax.axis_size("tile"))
    shift, radix = stages[0]
    keep = keep.reshape(radix, -1, n)
    got = got.reshape(keep.shape)
    rows = keep.shape[1]
    own, *sends = call(
        functools.partial(first_kernel, (shift, radix)),
        (((rows, n), f32),) + (((rows, n), bf16),) * (radix - 1),
        keep, got,
    )
    for at, (shift, radix) in enumerate(stages):
        got = [flipped(part, (k + 1) << shift) for k, part in enumerate(sends)]
        if at + 1 < len(stages):
            place = stages[at + 1]
            small = rows // place[1]
            outs = (((small, n), f32),) + (((small, n), bf16),) * (place[1] - 1)
        else:
            place, small = (0, 1), rows
            outs = (((rows, n), bf16),)
        own, *sends = call(
            functools.partial(stage_kernel, radix, place),
            outs, own, *got,
            scratch=[pltpu.VMEM((rows, n), f32)],
        )
        rows = small
    for at, (shift, radix) in reversed(list(enumerate(stages))):
        got = [flipped(own, k << shift) for k in range(1, radix)]
        if at:
            outs = (((rows * radix, n), bf16),)
            join = functools.partial(join_kernel, (shift, radix))
            (own,) = call(join, outs, own, *got)
            rows = rows * radix
    return (own, *got)


def probe_step(rate, probe, pieces):
    place = digits(lax.axis_size("tile"))[0]
    chunks = probe.reshape(place[1], -1, probe.shape[-1])
    (out,) = call(
        functools.partial(apply_kernel, rate, place),
        ((chunks.shape, f32),), chunks, *pieces,
    )
    return out.reshape(probe.shape)


def steps(obj, probe, mode_weights, measured, corner, counts, weight_index):
    n = probe.shape[-1]
    t = obj.shape[-1]
    tall, wide = dft_tables(n)
    rate = step_probe / (POS_DEV * lax.axis_size("tile"))
    state, half, rest, *edges = enter(obj[0], n)
    pm = probe
    po = swapped(probe)
    wm = mode_weights.T
    wo = swapped(wm)
    spots = corner.T
    meas = sort(measured, tall, wide)
    for sweep in range(ITERS):
        low = shifted(edges[1], -GC)
        diag = shifted(edges[2], -(GC + 1))
        right = shifted(edges[0], -1)
        mine = (half, right, low, diag)
        other = (rest, swapped(right), swapped(low), swapped(diag))
        own_keep, own_send, edge_keep, edge_send, pgm, pgo = patches(
            counts, spots, weight_index, wm, wo, mine, other, meas, pm, po, tall, wide
        )
        edge_got = swapped(edge_send)
        right, low, diag = margins(edge_keep, edge_got, t, n)
        low = shifted(low, GC)
        diag = shifted(diag, GC + 1)
        right = shifted(right, 1)
        pieces = probe_sum(pgm, swapped(pgo))
        own_got = swapped(own_send)
        state, half, *edges = update(state, own_keep, own_got, right, low, diag)
        pm = probe_step(rate, pm, pieces)
        if sweep < ITERS - 1:
            rest = swapped(half)
            others = [swapped(piece) for piece in pieces]
            po = probe_step(rate, po, others)
    return (leave(state, swapped(state))[None], pm)


def solution(mesh):
    placed = (
        P("tile", None, None, None),
        P("mode", None, None, None),
        P(None, "mode"),
        P("tile", None, None),
        P("tile", None),
        P("tile"),
        P("tile"),
    )
    return jax.shard_map(
        steps,
        mesh=mesh,
        in_specs=placed,
        out_specs=(P("tile", None, None, None), P("mode", None, None, None)),
        check_vma=False,
    )
```

```python
import functools
import math

import jax
import jax.numpy as jnp
from jax import lax
from jax.experimental import pallas as pl
from jax.experimental.pallas import tpu as pltpu
from jax.sharding import PartitionSpec as P


GC = 8
POS_DEV = 2
ITERS = 2
STRIP = 32

step_object = 0.1
step_probe = 4.0

f32 = jnp.float32
bf16 = jnp.bfloat16
VM = pl.BlockSpec(memory_space=pltpu.VMEM)
SM = pl.BlockSpec(memory_space=pltpu.SMEM)


def shifted(array, by):
    peers = lax.axis_size("tile")
    return lax.ppermute(array, "tile", [(i, (i + by) % peers) for i in range(peers)])


def flipped(array, mask):
    peers = lax.axis_size("tile")
    return lax.ppermute(array, "tile", [(i, i ^ mask) for i in range(peers)])


def swapped(array):
    return lax.ppermute(array, "mode", [(0, 1), (1, 0)])


def dft_tables(length):
    half = jnp.arange(length // 2, dtype=jnp.int32)
    factor = 1.0 / math.sqrt(length)
    tall, wide = [], []
    for parity in (0, 1):
        product = (2 * half[:, None] + parity) * half[None, :] % length
        for value, out in ((product, tall), (product.T, wide)):
            angle = value.astype(f32) * (2.0 * math.pi / length)
            real = jnp.cos(angle) * factor
            imag = -(jnp.sin(angle) * factor)
            if out is tall:
                rows = [[real, -imag], [imag, real]]
            else:
                rows = [[real, imag], [-imag, real]]
            out.append(jnp.concatenate([jnp.concatenate(row, 1) for row in rows], 0))
    return jnp.stack(tall).astype(bf16), jnp.stack(wide).astype(bf16)


def dot(a, b):
    return jnp.dot(a, b, preferred_element_type=f32)


LANES = 128
SUBS = 8


def blocks(t, n, refs):
    right, low, diag = refs
    return ((right, 0, t, t, n), (low, t, 0, n, t), (diag, t, t, n, n))


def packed_rows(t, n):
    return (t * n // LANES, n * t // LANES, n * n // LANES)


def patch_kernel(
    live, corner, kind, wm, wo,
    tm, rm, bm, dm, to, ro, bo, do, meas, pm, po, tall, wide_table,
    grad, own_send, edge_send, acc, pgo,
    frame, psi, xs, ts, orr, oii, term,
):
    n = pm.shape[-1]
    t = tm.shape[-1]
    half = pm.shape[0]
    modes = 2 * half
    me = lax.axis_index("mode")
    h = n // 2
    for plane, (a, b, c, d) in ((me, (tm, rm, bm, dm)), (1 - me, (to, ro, bo, do))):
        frame[plane, pl.ds(0, t), pl.ds(0, t)] = a[...].astype(f32)
        for ref, top, left, high, wide in blocks(t, n, (b, c, d)):
            for k in range(wide // LANES):
                part = ref[pl.ds(k * high, high), :].astype(f32)
                frame[plane, pl.ds(top, high), pl.ds(left + k * LANES, LANES)] = part
    grad[...] = jnp.zeros_like(grad)
    acc[...] = jnp.zeros_like(acc)

    def probe_at(m, c, rows, cols=slice(None)):
        ref = pm if m < half else po
        return ref[m % half, c, rows, cols]

    def slot_body(g, carry):
        s = me + 2 * g

        @pl.when(s < live[0])
        def _():
            row = corner[0, s]
            col = corner[1, s]
            cb = pl.multiple_of(col // LANES * LANES, LANES)
            cc = col - cb
            rb = pl.multiple_of(row // SUBS * SUBS, SUBS)
            rr = row - rb
            count, tall_count = n // LANES, n // SUBS
            lane = lax.broadcasted_iota(jnp.int32, (1, SUBS, LANES), 2)
            sub = lax.broadcasted_iota(jnp.int32, (1, SUBS, LANES), 1)
            rows = pl.ds(rb, n + SUBS)
            left, above = lane < LANES - cc, sub < SUBS - rr
            for p, out in ((0, orr), (1, oii)):
                turned = []
                for k in range(count + 1):
                    block = frame[p, rows, pl.ds(cb + k * LANES, LANES)]
                    block = block.reshape(tall_count + 1, SUBS, LANES)
                    turned.append(pltpu.roll(block, lax.rem(LANES - cc, LANES), 2))
                for k in range(count):
                    block = jnp.where(left, turned[k], turned[k + 1])
                    block = pltpu.roll(block, lax.rem(SUBS - rr, SUBS), 1)
                    block = jnp.where(above, block[:-1], block[1:])
                    out[:, pl.ds(k * LANES, LANES)] = block.reshape(n, LANES)
            lanes = [pl.ds(q * h, h) for q in range(2)]
            w = [wm[m, kind[s]] if m < half else wo[m - half, kind[s]] for m in range(modes)]
            for m in range(modes):
                for i in range(h // STRIP):
                    up, low = pl.ds(i * STRIP, STRIP), pl.ds(h + i * STRIP, STRIP)
                    parts = []
                    for rows in (up, low):
                        a, b = orr[rows, :], oii[rows, :]
                        pr, pi = probe_at(m, 0, rows), probe_at(m, 1, rows)
                        parts.append((pr * a - pi * b, pr * b + pi * a))
                    (r0, i0), (r1, i1) = parts
                    xs[m, 0, up, :] = (r0 + r1).astype(bf16)
                    xs[m, 0, low, :] = (i0 + i1).astype(bf16)
                    xs[m, 1, up, :] = (r0 - r1).astype(bf16)
                    xs[m, 1, low, :] = (i0 - i1).astype(bf16)
            for m in range(modes):
                for p in range(2):
                    y = dot(tall[p], xs[m, p])
                    rows = pl.ds(m * n + p * h, h)
                    for c in range(2):
                        part = y[c * h : (c + 1) * h]
                        ts[0, rows, lanes[c]] = (part[:, :h] + part[:, h:]).astype(bf16)
                        ts[1, rows, lanes[c]] = (part[:, :h] - part[:, h:]).astype(bf16)
            for q in range(2):
                psi[q] = dot(ts[q], wide_table[q])
            for i in range(n // STRIP):
                p, base = divmod(i * STRIP, h)
                for q in range(2):
                    total = jnp.zeros((STRIP, h), f32)
                    for m in range(modes):
                        rows = pl.ds(m * n + i * STRIP, STRIP)
                        a, b = psi[q, rows, lanes[0]], psi[q, rows, lanes[1]]
                        total = total + w[m] * (a * a + b * b)
                    resid = total - meas[g, pl.ds(i * STRIP, STRIP), lanes[q]]
                    for m in range(modes):
                        rows = pl.ds(m * n + i * STRIP, STRIP)
                        scale = w[m] * resid
                        for c in range(2):
                            value = scale * psi[q, rows, lanes[c]]
                            xs[m, p, pl.ds(c * h + base, STRIP), lanes[q]] = value.astype(bf16)
            for m in range(modes):
                even = dot(wide_table[0], xs[m, 0])
                odd = dot(wide_table[1], xs[m, 1])
                for side, y in enumerate((even + odd, even - odd)):
                    rows = pl.ds(m * n + side * h, h)
                    for c in range(2):
                        part = y[c * h : (c + 1) * h].astype(bf16)
                        ts[0, rows, lanes[c]] = part[:, :h]
                        ts[1, rows, lanes[c]] = part[:, h:]
            for q in range(2):
                psi[q] = dot(ts[q], tall[q])
            for i in range(n // STRIP):
                up = pl.ds(i * STRIP, STRIP)
                for side in range(2):
                    cols = lanes[side]
                    a, b = orr[up, cols], oii[up, cols]
                    tr = jnp.zeros((STRIP, h), f32)
                    ti = jnp.zeros((STRIP, h), f32)
                    for m in range(modes):
                        rows = pl.ds(m * n + i * STRIP, STRIP)
                        sums = []
                        for c in range(2):
                            first, second = psi[0, rows, lanes[c]], psi[1, rows, lanes[c]]
                            sums.append(first - second if side else first + second)
                        cr, ci = sums
                        pr, pi = probe_at(m, 0, up, cols), probe_at(m, 1, up, cols)
                        tr = tr + (pr * cr + pi * ci)
                        ti = ti + (pr * ci - pi * cr)
                        acc[m, 0, up, cols] += a * cr + b * ci
                        acc[m, 1, up, cols] += a * ci - b * cr
                    term[0, up, cols] = tr
                    term[1, up, cols] = ti
            rows = pl.ds(rb, n + SUBS)
            begun, over = lane < cc, sub < rr
            for p in range(2):
                turned = []
                for k in range(count):
                    block = term[p, :, pl.ds(k * LANES, LANES)]
                    block = pltpu.roll(block.reshape(tall_count, SUBS, LANES), rr, 1)
                    edge = jnp.zeros((1, SUBS, LANES), f32)
                    before = jnp.concatenate([edge, block], 0)
                    after = jnp.concatenate([block, edge], 0)
                    turned.append(pltpu.roll(jnp.where(over, before, after), cc, 2))
                nothing = jnp.zeros_like(turned[0])
                for k in range(count + 1):
                    low = turned[k - 1] if k else nothing
                    high = turned[k] if k < count else nothing
                    cols = pl.ds(cb + k * LANES, LANES)
                    moved = jnp.where(begun, low, high)
                    grad[p, rows, cols] += moved.reshape(n + SUBS, LANES)

        return carry

    lax.fori_loop(0, meas.shape[0], slot_body, 0)
    own_send[...] = grad[1 - me, pl.ds(0, t), pl.ds(0, t)].astype(bf16)
    base = 0
    for _, top, left, high, wide in blocks(t, n, (None,) * 3):
        for k in range(wide // LANES):
            rows, lanes = pl.ds(top, high), pl.ds(left + k * LANES, LANES)
            edge_send[pl.ds(base, high), :] = grad[1 - me, rows, lanes].astype(bf16)
            base += high
    for m in range(half):
        pgo[m] = acc[half + m].astype(bf16)


def call(kernel, outs, *args, smem=0, scratch=(), limit=4 * 1024 * 1024):
    return pl.pallas_call(
        kernel,
        out_shape=tuple(jax.ShapeDtypeStruct(shape, dtype) for shape, dtype in outs),
        in_specs=[SM] * smem + [VM] * (len(args) - smem),
        out_specs=(VM,) * len(outs),
        scratch_shapes=list(scratch),
        compiler_params=pltpu.CompilerParams(vmem_limit_bytes=limit),
        name="kernel",
    )(*args)


def sort_kernel(meas, tall, wide, out):
    me = lax.axis_index("mode")
    n = out.shape[-1]
    h = n // 2
    row = lax.broadcasted_iota(jnp.int32, (n, n), 0)
    col = lax.broadcasted_iota(jnp.int32, (n, n), 1)

    def source(i):
        return jnp.where(i < h, 2 * i, 2 * i - (n - 1))

    def exact(product, value):
        total = jnp.zeros_like(value)
        for _ in range(3):
            part = value.astype(bf16)
            total = total + product(part)
            value = value - part.astype(f32)
        return total

    right = (row == source(col)).astype(f32).astype(bf16)
    left = (col == source(row)).astype(f32).astype(bf16)
    for g in range(out.shape[0]):
        value = exact(lambda part: dot(part, right), meas[me + 2 * g])
        out[g] = exact(lambda part: dot(left, part), value)


def sort(meas, tall, wide):
    outs = (((meas.shape[0] // 2, *meas.shape[1:]), f32),)
    return call(sort_kernel, outs, meas, tall, wide)[0]


def patches(live, corner, kind, wm, wo, mine, other, meas, pm, po, tall, wide):
    n = pm.shape[-1]
    t = mine[0].shape[-1]
    f = n + t
    modes = 2 * pm.shape[0]
    rows = sum(packed_rows(t, n))
    return call(
        patch_kernel,
        (
            ((2, f, f), f32),
            ((t, t), bf16),
            ((rows, LANES), bf16),
            ((modes, *pm.shape[1:]), f32),
            (pm.shape, bf16),
        ),
        live, corner, kind, wm, wo, *mine, *other, meas, pm, po, tall, wide,
        smem=5,
        scratch=[
            pltpu.VMEM((2, f, f), f32),
            pltpu.VMEM((2, modes * n, n), f32),
            pltpu.VMEM((modes, 2, n, n), bf16),
            pltpu.VMEM((2, modes * n, n), bf16),
            pltpu.VMEM((n, n), f32),
            pltpu.VMEM((n, n), f32),
            pltpu.VMEM((2, n, n), f32),
        ],
        limit=20 * 1024 * 1024,
    )


def pack_edges(value, t, n, outs):
    for out, _, _, high, wide in blocks(t, n, outs):
        for k in range(wide // LANES):
            out[pl.ds(k * high, high), :] = value[:high, k * LANES : (k + 1) * LANES]


def enter_kernel(obj, state, half, rest, hr, hl, hd):
    me = lax.axis_index("mode")
    t = obj.shape[-1]
    n = hl.shape[0] * LANES // t
    value = obj[me]
    state[...] = value
    small = value.astype(bf16)
    half[...] = small
    pack_edges(small, t, n, (hr, hl, hd))
    rest[...] = obj[1 - me].astype(bf16)


def edge_shapes(t, n):
    return tuple(((rows, LANES), bf16) for rows in packed_rows(t, n))


def enter(obj, n):
    t = obj.shape[-1]
    outs = (((t, t), f32), ((t, t), bf16), ((t, t), bf16)) + edge_shapes(t, n)
    return call(enter_kernel, outs, obj)


def margin_kernel(t, n, grad, got, right, low, diag):
    me = lax.axis_index("mode")
    base = 0
    for out, top, left, high, wide in blocks(t, n, (right, low, diag)):
        for k in range(wide // LANES):
            value = grad[me, pl.ds(top, high), pl.ds(left + k * LANES, LANES)]
            value = value + got[pl.ds(base, high), :].astype(f32)
            out[pl.ds(k * high, high), :] = value.astype(bf16)
            base += high


def margins(grad, got, t, n):
    kernel = functools.partial(margin_kernel, t, n)
    return call(kernel, edge_shapes(t, n), grad, got)


def update_kernel(state, grad, got, right, low, diag, new, half, hr, hl, hd):
    t = state.shape[0]
    n = low.shape[0] * LANES // t
    own = grad[lax.axis_index("mode"), pl.ds(0, t), pl.ds(0, t)]
    new[...] = own + got[...].astype(f32)
    for ref, _, _, high, wide in blocks(t, n, (right, low, diag)):
        for k in range(wide // LANES):
            lanes = pl.ds(k * LANES, LANES)
            new[pl.ds(0, high), lanes] += ref[pl.ds(k * high, high), :].astype(f32)
    value = state[...] - step_object * new[...]
    new[...] = value
    small = value.astype(bf16)
    half[...] = small
    pack_edges(small, t, n, (hr, hl, hd))


def update(state, keep, got, right, low, diag):
    t = state.shape[0]
    n = low.shape[0] * LANES // t
    outs = (((t, t), f32), ((t, t), bf16)) + edge_shapes(t, n)
    return call(update_kernel, outs, state, keep, got, right, low, diag)


def leave_kernel(state, rest, out):
    me = lax.axis_index("mode")
    out[me] = state[...]
    out[1 - me] = rest[...]


def leave(state, rest):
    outs = (((2, *state.shape), f32),)
    return call(leave_kernel, outs, state, rest)[0]


def digits(peers):
    out, shift = [], 0
    while 1 << shift < peers:
        radix = 4 if (4 << shift) <= peers else 2
        out.append((shift, radix))
        shift += radix.bit_length() - 1
    return out


def spot_of(shift, radix):
    return (lax.axis_index("tile") >> shift) & (radix - 1)


def first_kernel(place, keep, got, own, *sends):
    i = spot_of(*place)
    own[...] = keep[i] + got[i].astype(f32)
    for k, out in enumerate(sends):
        j = i ^ (k + 1)
        out[...] = (keep[j] + got[j].astype(f32)).astype(bf16)


def stage_kernel(before, place, have, *refs):
    after = place[1]
    got = refs[: before - 1]
    own, sends = refs[before - 1], refs[before:]
    total = refs[-1]
    sends = sends[:-1]
    value = have[...]
    for ref in got:
        value = value + ref[...].astype(f32)
    if after == 1:
        own[...] = value.astype(bf16)
        return
    total[...] = value
    rows = own.shape[0]
    i = spot_of(*place)
    own[...] = total[pl.ds(pl.multiple_of(i * rows, rows), rows), :]
    for k, out in enumerate(sends):
        j = i ^ (k + 1)
        out[...] = total[pl.ds(pl.multiple_of(j * rows, rows), rows), :].astype(bf16)


def join_kernel(place, have, *refs):
    got, out = refs[:-1], refs[-1]
    rows = have.shape[0]
    i = spot_of(*place)
    out[pl.ds(pl.multiple_of(i * rows, rows), rows), :] = have[...]
    for k, ref in enumerate(got):
        j = i ^ (k + 1)
        out[pl.ds(pl.multiple_of(j * rows, rows), rows), :] = ref[...]


def apply_kernel(rate, place, probe, have, *refs):
    got, out = refs[:-1], refs[-1]
    i = spot_of(*place)
    for k, ref in enumerate((have, *got)):
        j = i ^ k
        out[j] = probe[j] - rate * ref[...].astype(f32)


def probe_sum(keep, got):
    n = keep.shape[-1]
    stages = digits(lax.axis_size("tile"))
    shift, radix = stages[0]
    got = got.reshape(radix, -1, n)
    rows = got.shape[1]
    keep = keep.reshape(-1, rows, n)
    own, *sends = call(
        functools.partial(first_kernel, (shift, radix)),
        (((rows, n), f32),) + (((rows, n), bf16),) * (radix - 1),
        keep, got,
    )
    for at, (shift, radix) in enumerate(stages):
        got = [flipped(part, (k + 1) << shift) for k, part in enumerate(sends)]
        if at + 1 < len(stages):
            place = stages[at + 1]
            small = rows // place[1]
            outs = (((small, n), f32),) + (((small, n), bf16),) * (place[1] - 1)
        else:
            place, small = (0, 1), rows
            outs = (((rows, n), bf16),)
        own, *sends = call(
            functools.partial(stage_kernel, radix, place),
            outs, own, *got,
            scratch=[pltpu.VMEM((rows, n), f32)],
        )
        rows = small
    for at, (shift, radix) in reversed(list(enumerate(stages))):
        got = [flipped(own, k << shift) for k in range(1, radix)]
        if at:
            outs = (((rows * radix, n), bf16),)
            join = functools.partial(join_kernel, (shift, radix))
            (own,) = call(join, outs, own, *got)
            rows = rows * radix
    return (own, *got)


def probe_step(rate, probe, pieces):
    place = digits(lax.axis_size("tile"))[0]
    chunks = probe.reshape(place[1], -1, probe.shape[-1])
    (out,) = call(
        functools.partial(apply_kernel, rate, place),
        ((chunks.shape, f32),), chunks, *pieces,
    )
    return out.reshape(probe.shape)


def steps(obj, probe, mode_weights, measured, corner, counts, weight_index):
    n = probe.shape[-1]
    t = obj.shape[-1]
    tall, wide = dft_tables(n)
    rate = step_probe / (POS_DEV * lax.axis_size("tile"))
    state, half, rest, *edges = enter(obj[0], n)
    pm = probe
    po = swapped(probe)
    wm = mode_weights.T
    wo = swapped(wm)
    spots = corner.T
    meas = sort(measured, tall, wide)
    for sweep in range(ITERS):
        low = shifted(edges[1], -GC)
        diag = shifted(edges[2], -(GC + 1))
        right = shifted(edges[0], -1)
        mine = (half, right, low, diag)
        other = (rest, swapped(right), swapped(low), swapped(diag))
        grad, own_send, edge_send, acc, pgo = patches(
            counts, spots, weight_index, wm, wo, mine, other, meas, pm, po, tall, wide
        )
        edge_got = swapped(edge_send)
        right, low, diag = margins(grad, edge_got, t, n)
        low = shifted(low, GC)
        diag = shifted(diag, GC + 1)
        right = shifted(right, 1)
        pieces = probe_sum(acc, swapped(pgo))
        own_got = swapped(own_send)
        state, half, *edges = update(state, grad, own_got, right, low, diag)
        pm = probe_step(rate, pm, pieces)
        if sweep < ITERS - 1:
            rest = swapped(half)
            others = [swapped(piece) for piece in pieces]
            po = probe_step(rate, po, others)
    return (leave(state, swapped(state))[None], pm)


def solution(mesh):
    placed = (
        P("tile", None, None, None),
        P("mode", None, None, None),
        P(None, "mode"),
        P("tile", None, None),
        P("tile", None),
        P("tile"),
        P("tile"),
    )
    return jax.shard_map(
        steps,
        mesh=mesh,
        in_specs=placed,
        out_specs=(P("tile", None, None, None), P("mode", None, None, None)),
        check_vma=False,
    )
```

```python
import functools
import math

import jax
import jax.numpy as jnp
from jax import lax
from jax.experimental import pallas as pl
from jax.experimental.pallas import tpu as pltpu
from jax.sharding import PartitionSpec as P


GC = 8
POS_DEV = 2
ITERS = 2
STRIP = 32

step_object = 0.1
step_probe = 4.0

f32 = jnp.float32
bf16 = jnp.bfloat16
VM = pl.BlockSpec(memory_space=pltpu.VMEM)
SM = pl.BlockSpec(memory_space=pltpu.SMEM)


def shifted(array, by):
    peers = lax.axis_size("tile")
    return lax.ppermute(array, "tile", [(i, (i + by) % peers) for i in range(peers)])


def flipped(array, mask):
    peers = lax.axis_size("tile")
    return lax.ppermute(array, "tile", [(i, i ^ mask) for i in range(peers)])


def swapped(array):
    return lax.ppermute(array, "mode", [(0, 1), (1, 0)])


def dft_tables(length):
    half = jnp.arange(length // 2, dtype=jnp.int32)
    factor = 1.0 / math.sqrt(length)
    tall, wide = [], []
    for parity in (0, 1):
        product = (2 * half[:, None] + parity) * half[None, :] % length
        for value, out in ((product, tall), (product.T, wide)):
            angle = value.astype(f32) * (2.0 * math.pi / length)
            real = jnp.cos(angle) * factor
            imag = -(jnp.sin(angle) * factor)
            if out is tall:
                rows = [[real, -imag], [imag, real]]
            else:
                rows = [[real, imag], [-imag, real]]
            out.append(jnp.concatenate([jnp.concatenate(row, 1) for row in rows], 0))
    return jnp.stack(tall).astype(bf16), jnp.stack(wide).astype(bf16)


def dot(a, b):
    return jnp.dot(a, b, preferred_element_type=f32)


LANES = 128
SUBS = 8


def blocks(t, n, refs):
    right, low, diag = refs
    return ((right, 0, t, t, n), (low, t, 0, n, t), (diag, t, t, n, n))


def packed_rows(t, n):
    return (t * n // LANES, n * t // LANES, n * n // LANES)


def patch_kernel(
    live, corner, kind, wm, wo,
    tm, rm, bm, dm, to, ro, bo, do, meas, pm, po, tall, wide_table,
    grad, own_send, edge_send, acc, pgo,
    frame, psi, xs, ts, orr, oii, term,
):
    n = pm.shape[-1]
    t = tm.shape[-1]
    half = pm.shape[0]
    modes = 2 * half
    me = lax.axis_index("mode")
    h = n // 2
    for plane, (a, b, c, d) in ((me, (tm, rm, bm, dm)), (1 - me, (to, ro, bo, do))):
        frame[plane, pl.ds(0, t), pl.ds(0, t)] = a[...].astype(f32)
        for ref, top, left, high, wide in blocks(t, n, (b, c, d)):
            for k in range(wide // LANES):
                part = ref[pl.ds(k * high, high), :].astype(f32)
                frame[plane, pl.ds(top, high), pl.ds(left + k * LANES, LANES)] = part
    grad[...] = jnp.zeros_like(grad)
    acc[...] = jnp.zeros_like(acc)

    def probe_at(m, c, rows, cols=slice(None)):
        ref = pm if m < half else po
        return ref[m % half, c, rows, cols]

    def slot_body(g, carry):
        s = me + 2 * g

        @pl.when(s < live[0])
        def _():
            row = corner[0, s]
            col = corner[1, s]
            cb = pl.multiple_of(col // LANES * LANES, LANES)
            cc = col - cb
            rb = pl.multiple_of(row // SUBS * SUBS, SUBS)
            rr = row - rb
            count, tall_count = n // LANES, n // SUBS
            lane = lax.broadcasted_iota(jnp.int32, (1, SUBS, LANES), 2)
            sub = lax.broadcasted_iota(jnp.int32, (1, SUBS, LANES), 1)
            rows = pl.ds(rb, n + SUBS)
            left, above = lane < LANES - cc, sub < SUBS - rr
            for p, out in ((0, orr), (1, oii)):
                turned = []
                for k in range(count + 1):
                    block = frame[p, rows, pl.ds(cb + k * LANES, LANES)]
                    block = block.reshape(tall_count + 1, SUBS, LANES)
                    turned.append(pltpu.roll(block, lax.rem(LANES - cc, LANES), 2))
                for k in range(count):
                    block = jnp.where(left, turned[k], turned[k + 1])
                    block = pltpu.roll(block, lax.rem(SUBS - rr, SUBS), 1)
                    block = jnp.where(above, block[:-1], block[1:])
                    out[:, pl.ds(k * LANES, LANES)] = block.reshape(n, LANES)
            lanes = [pl.ds(q * h, h) for q in range(2)]
            w = [wm[m, kind[s]] if m < half else wo[m - half, kind[s]] for m in range(modes)]
            for m in range(modes):
                for i in range(h // STRIP):
                    up, low = pl.ds(i * STRIP, STRIP), pl.ds(h + i * STRIP, STRIP)
                    parts = []
                    for rows in (up, low):
                        a, b = orr[rows, :], oii[rows, :]
                        pr, pi = probe_at(m, 0, rows), probe_at(m, 1, rows)
                        parts.append((pr * a - pi * b, pr * b + pi * a))
                    (r0, i0), (r1, i1) = parts
                    xs[m, 0, up, :] = (r0 + r1).astype(bf16)
                    xs[m, 0, low, :] = (i0 + i1).astype(bf16)
                    xs[m, 1, up, :] = (r0 - r1).astype(bf16)
                    xs[m, 1, low, :] = (i0 - i1).astype(bf16)
            for m in range(modes):
                for p in range(2):
                    y = dot(tall[p], xs[m, p])
                    rows = pl.ds(m * n + p * h, h)
                    for c in range(2):
                        part = y[c * h : (c + 1) * h]
                        ts[0, rows, lanes[c]] = (part[:, :h] + part[:, h:]).astype(bf16)
                        ts[1, rows, lanes[c]] = (part[:, :h] - part[:, h:]).astype(bf16)
            for q in range(2):
                psi[q] = dot(ts[q], wide_table[q])
            for i in range(n // STRIP):
                p, base = divmod(i * STRIP, h)
                for q in range(2):
                    total = jnp.zeros((STRIP, h), f32)
                    for m in range(modes):
                        rows = pl.ds(m * n + i * STRIP, STRIP)
                        a, b = psi[q, rows, lanes[0]], psi[q, rows, lanes[1]]
                        total = total + w[m] * (a * a + b * b)
                    resid = total - meas[g, pl.ds(i * STRIP, STRIP), lanes[q]]
                    for m in range(modes):
                        rows = pl.ds(m * n + i * STRIP, STRIP)
                        scale = w[m] * resid
                        for c in range(2):
                            value = scale * psi[q, rows, lanes[c]]
                            xs[m, p, pl.ds(c * h + base, STRIP), lanes[q]] = value.astype(bf16)
            for m in range(modes):
                even = dot(wide_table[0], xs[m, 0])
                odd = dot(wide_table[1], xs[m, 1])
                for side, y in enumerate((even + odd, even - odd)):
                    rows = pl.ds(m * n + side * h, h)
                    for c in range(2):
                        part = y[c * h : (c + 1) * h].astype(bf16)
                        ts[0, rows, lanes[c]] = part[:, :h]
                        ts[1, rows, lanes[c]] = part[:, h:]
            for q in range(2):
                psi[q] = dot(ts[q], tall[q])
            for i in range(n // STRIP):
                up = pl.ds(i * STRIP, STRIP)
                for side in range(2):
                    cols = lanes[side]
                    a, b = orr[up, cols], oii[up, cols]
                    tr = jnp.zeros((STRIP, h), f32)
                    ti = jnp.zeros((STRIP, h), f32)
                    for m in range(modes):
                        rows = pl.ds(m * n + i * STRIP, STRIP)
                        sums = []
                        for c in range(2):
                            first, second = psi[0, rows, lanes[c]], psi[1, rows, lanes[c]]
                            sums.append(first - second if side else first + second)
                        cr, ci = sums
                        pr, pi = probe_at(m, 0, up, cols), probe_at(m, 1, up, cols)
                        tr = tr + (pr * cr + pi * ci)
                        ti = ti + (pr * ci - pi * cr)
                        acc[m, 0, up, cols] += a * cr + b * ci
                        acc[m, 1, up, cols] += a * ci - b * cr
                    term[0, up, cols] = tr
                    term[1, up, cols] = ti
            rows = pl.ds(rb, n + SUBS)
            begun, over = lane < cc, sub < rr
            for p in range(2):
                turned = []
                for k in range(count):
                    block = term[p, :, pl.ds(k * LANES, LANES)]
                    block = pltpu.roll(block.reshape(tall_count, SUBS, LANES), rr, 1)
                    edge = jnp.zeros((1, SUBS, LANES), f32)
                    before = jnp.concatenate([edge, block], 0)
                    after = jnp.concatenate([block, edge], 0)
                    turned.append(pltpu.roll(jnp.where(over, before, after), cc, 2))
                nothing = jnp.zeros_like(turned[0])
                for k in range(count + 1):
                    low = turned[k - 1] if k else nothing
                    high = turned[k] if k < count else nothing
                    cols = pl.ds(cb + k * LANES, LANES)
                    moved = jnp.where(begun, low, high)
                    grad[p, rows, cols] += moved.reshape(n + SUBS, LANES)

        return carry

    lax.fori_loop(0, meas.shape[0], slot_body, 0)
    own_send[...] = grad[1 - me, pl.ds(0, t), pl.ds(0, t)].astype(bf16)
    base = 0
    for _, top, left, high, wide in blocks(t, n, (None,) * 3):
        for k in range(wide // LANES):
            rows, lanes = pl.ds(top, high), pl.ds(left + k * LANES, LANES)
            edge_send[pl.ds(base, high), :] = grad[1 - me, rows, lanes].astype(bf16)
            base += high
    for m in range(half):
        pgo[m] = acc[half + m].astype(bf16)


def call(kernel, outs, *args, smem=0, scratch=(), limit=4 * 1024 * 1024):
    return pl.pallas_call(
        kernel,
        out_shape=tuple(jax.ShapeDtypeStruct(shape, dtype) for shape, dtype in outs),
        in_specs=[SM] * smem + [VM] * (len(args) - smem),
        out_specs=(VM,) * len(outs),
        scratch_shapes=list(scratch),
        compiler_params=pltpu.CompilerParams(vmem_limit_bytes=limit),
        name="kernel",
    )(*args)


def sort_kernel(meas, tall, wide, out):
    me = lax.axis_index("mode")
    n = out.shape[-1]
    h = n // 2
    row = lax.broadcasted_iota(jnp.int32, (n, n), 0)
    col = lax.broadcasted_iota(jnp.int32, (n, n), 1)

    def source(i):
        return jnp.where(i < h, 2 * i, 2 * i - (n - 1))

    def exact(product, value):
        total = jnp.zeros_like(value)
        for _ in range(3):
            part = value.astype(bf16)
            total = total + product(part)
            value = value - part.astype(f32)
        return total

    right = (row == source(col)).astype(f32).astype(bf16)
    left = (col == source(row)).astype(f32).astype(bf16)
    for g in range(out.shape[0]):
        value = exact(lambda part: dot(part, right), meas[me + 2 * g])
        out[g] = exact(lambda part: dot(left, part), value)


def sort(meas, tall, wide):
    outs = (((meas.shape[0] // 2, *meas.shape[1:]), f32),)
    return call(sort_kernel, outs, meas, tall, wide)[0]


def patches(live, corner, kind, wm, wo, mine, other, meas, pm, po, tall, wide):
    n = pm.shape[-1]
    t = mine[0].shape[-1]
    f = n + t
    modes = 2 * pm.shape[0]
    rows = sum(packed_rows(t, n))
    return call(
        patch_kernel,
        (
            ((2, f, f), f32),
            ((t, t), bf16),
            ((rows, LANES), bf16),
            ((modes, *pm.shape[1:]), f32),
            (pm.shape, bf16),
        ),
        live, corner, kind, wm, wo, *mine, *other, meas, pm, po, tall, wide,
        smem=5,
        scratch=[
            pltpu.VMEM((2, f, f), f32),
            pltpu.VMEM((2, modes * n, n), f32),
            pltpu.VMEM((modes, 2, n, n), bf16),
            pltpu.VMEM((2, modes * n, n), bf16),
            pltpu.VMEM((n, n), f32),
            pltpu.VMEM((n, n), f32),
            pltpu.VMEM((2, n, n), f32),
        ],
        limit=20 * 1024 * 1024,
    )


def pack_edges(value, t, n, outs):
    for out, _, _, high, wide in blocks(t, n, outs):
        for k in range(wide // LANES):
            out[pl.ds(k * high, high), :] = value[:high, k * LANES : (k + 1) * LANES]


def enter_kernel(obj, state, half, rest, hr, hl, hd):
    me = lax.axis_index("mode")
    t = obj.shape[-1]
    n = hl.shape[0] * LANES // t
    value = obj[me]
    state[...] = value
    small = value.astype(bf16)
    half[...] = small
    pack_edges(small, t, n, (hr, hl, hd))
    rest[...] = obj[1 - me].astype(bf16)


def edge_shapes(t, n):
    return tuple(((rows, LANES), bf16) for rows in packed_rows(t, n))


def enter(obj, n):
    t = obj.shape[-1]
    outs = (((t, t), f32), ((t, t), bf16), ((t, t), bf16)) + edge_shapes(t, n)
    return call(enter_kernel, outs, obj)


def margin_kernel(t, n, grad, got, right, low, diag):
    me = lax.axis_index("mode")
    base = 0
    for out, top, left, high, wide in blocks(t, n, (right, low, diag)):
        for k in range(wide // LANES):
            value = grad[me, pl.ds(top, high), pl.ds(left + k * LANES, LANES)]
            value = value + got[pl.ds(base, high), :].astype(f32)
            out[pl.ds(k * high, high), :] = value.astype(bf16)
            base += high


def margins(grad, got, t, n):
    kernel = functools.partial(margin_kernel, t, n)
    return call(kernel, edge_shapes(t, n), grad, got)


def update_kernel(state, grad, got, right, low, diag, new, *smalls):
    t = state.shape[0]
    n = low.shape[0] * LANES // t
    own = grad[lax.axis_index("mode"), pl.ds(0, t), pl.ds(0, t)]
    new[...] = own + got[...].astype(f32)
    for ref, _, _, high, wide in blocks(t, n, (right, low, diag)):
        for k in range(wide // LANES):
            lanes = pl.ds(k * LANES, LANES)
            new[pl.ds(0, high), lanes] += ref[pl.ds(k * high, high), :].astype(f32)
    value = state[...] - step_object * new[...]
    new[...] = value
    if smalls:
        small = value.astype(bf16)
        smalls[0][...] = small
        pack_edges(small, t, n, smalls[1:])


def update(state, keep, got, right, low, diag, last):
    t = state.shape[0]
    n = low.shape[0] * LANES // t
    outs = (((t, t), f32), ((t, t), bf16)) + edge_shapes(t, n)
    if last:
        outs = outs[:1]
    return call(update_kernel, outs, state, keep, got, right, low, diag)


def leave_kernel(state, rest, out):
    me = lax.axis_index("mode")
    out[me] = state[...]
    out[1 - me] = rest[...]


def leave(state, rest):
    outs = (((2, *state.shape), f32),)
    return call(leave_kernel, outs, state, rest)[0]


def digits(peers):
    out, shift = [], 0
    while 1 << shift < peers:
        radix = 4 if (4 << shift) <= peers else 2
        out.append((shift, radix))
        shift += radix.bit_length() - 1
    return out


def spot_of(shift, radix):
    return (lax.axis_index("tile") >> shift) & (radix - 1)


def first_kernel(place, keep, got, own, *sends):
    i = spot_of(*place)
    own[...] = keep[i] + got[i].astype(f32)
    for k, out in enumerate(sends):
        j = i ^ (k + 1)
        out[...] = (keep[j] + got[j].astype(f32)).astype(bf16)


def stage_kernel(before, place, have, *refs):
    after = place[1]
    got = refs[: before - 1]
    own, sends = refs[before - 1], refs[before:]
    total = refs[-1]
    sends = sends[:-1]
    value = have[...]
    for ref in got:
        value = value + ref[...].astype(f32)
    if after == 1:
        own[...] = value.astype(bf16)
        return
    total[...] = value
    rows = own.shape[0]
    i = spot_of(*place)
    own[...] = total[pl.ds(pl.multiple_of(i * rows, rows), rows), :]
    for k, out in enumerate(sends):
        j = i ^ (k + 1)
        out[...] = total[pl.ds(pl.multiple_of(j * rows, rows), rows), :].astype(bf16)


def join_kernel(place, have, *refs):
    got, out = refs[:-1], refs[-1]
    rows = have.shape[0]
    i = spot_of(*place)
    out[pl.ds(pl.multiple_of(i * rows, rows), rows), :] = have[...]
    for k, ref in enumerate(got):
        j = i ^ (k + 1)
        out[pl.ds(pl.multiple_of(j * rows, rows), rows), :] = ref[...]


def apply_kernel(rate, place, probe, have, *refs):
    got, out = refs[:-1], refs[-1]
    i = spot_of(*place)
    for k, ref in enumerate((have, *got)):
        j = i ^ k
        out[j] = probe[j] - rate * ref[...].astype(f32)


def probe_sum(keep, got):
    n = keep.shape[-1]
    stages = digits(lax.axis_size("tile"))
    shift, radix = stages[0]
    got = got.reshape(radix, -1, n)
    rows = got.shape[1]
    keep = keep.reshape(-1, rows, n)
    own, *sends = call(
        functools.partial(first_kernel, (shift, radix)),
        (((rows, n), f32),) + (((rows, n), bf16),) * (radix - 1),
        keep, got,
    )
    for at, (shift, radix) in enumerate(stages):
        got = [flipped(part, (k + 1) << shift) for k, part in enumerate(sends)]
        if at + 1 < len(stages):
            place = stages[at + 1]
            small = rows // place[1]
            outs = (((small, n), f32),) + (((small, n), bf16),) * (place[1] - 1)
        else:
            place, small = (0, 1), rows
            outs = (((rows, n), bf16),)
        own, *sends = call(
            functools.partial(stage_kernel, radix, place),
            outs, own, *got,
            scratch=[pltpu.VMEM((rows, n), f32)],
        )
        rows = small
    for at, (shift, radix) in reversed(list(enumerate(stages))):
        got = [flipped(own, k << shift) for k in range(1, radix)]
        if at:
            outs = (((rows * radix, n), bf16),)
            join = functools.partial(join_kernel, (shift, radix))
            (own,) = call(join, outs, own, *got)
            rows = rows * radix
    return (own, *got)


def probe_step(rate, probe, pieces):
    place = digits(lax.axis_size("tile"))[0]
    chunks = probe.reshape(place[1], -1, probe.shape[-1])
    (out,) = call(
        functools.partial(apply_kernel, rate, place),
        ((chunks.shape, f32),), chunks, *pieces,
    )
    return out.reshape(probe.shape)


def steps(obj, probe, mode_weights, measured, corner, counts, weight_index):
    n = probe.shape[-1]
    t = obj.shape[-1]
    tall, wide = dft_tables(n)
    rate = step_probe / (POS_DEV * lax.axis_size("tile"))
    state, half, rest, *edges = enter(obj[0], n)
    pm = probe
    po = swapped(probe)
    wm = mode_weights.T
    wo = swapped(wm)
    spots = corner.T
    meas = sort(measured, tall, wide)
    for sweep in range(ITERS):
        low = shifted(edges[1], -GC)
        diag = shifted(edges[2], -(GC + 1))
        right = shifted(edges[0], -1)
        mine = (half, right, low, diag)
        other = (rest, swapped(right), swapped(low), swapped(diag))
        grad, own_send, edge_send, acc, pgo = patches(
            counts, spots, weight_index, wm, wo, mine, other, meas, pm, po, tall, wide
        )
        edge_got = swapped(edge_send)
        right, low, diag = margins(grad, edge_got, t, n)
        low = shifted(low, GC)
        diag = shifted(diag, GC + 1)
        right = shifted(right, 1)
        pieces = probe_sum(acc, swapped(pgo))
        own_got = swapped(own_send)
        last = sweep == ITERS - 1
        state, *after = update(state, grad, own_got, right, low, diag, last)
        pm = probe_step(rate, pm, pieces)
        if not last:
            half, *edges = after
            rest = swapped(half)
            others = [swapped(piece) for piece in pieces]
            po = probe_step(rate, po, others)
    return (leave(state, swapped(state))[None], pm)


def solution(mesh):
    placed = (
        P("tile", None, None, None),
        P("mode", None, None, None),
        P(None, "mode"),
        P("tile", None, None),
        P("tile", None),
        P("tile"),
        P("tile"),
    )
    return jax.shard_map(
        steps,
        mesh=mesh,
        in_specs=placed,
        out_specs=(P("tile", None, None, None), P("mode", None, None, None)),
        check_vma=False,
    )
```
